512 devices in a mesh: section: 16 (over x_lo, z), dp: 16 (over y, x_hi), hid: 2 (over core).
Axes of the slice: x: 4 (x_hi: 2, x_lo: 2; x = x_hi * 2 + x_lo), y: 8, z: 8, core: 2. Of those that a mesh axis runs over, the one named last changes fastest.
Arguments:
- forward_input: bfloat16 [16, 3072, 2048], P('section', 'dp'), may hold values from -6 to 6
- backward_input: bfloat16 [16, 3072, 2048], P('section', 'dp'), may hold values from -6 to 6
- output_grad: bfloat16 [16, 3072, 2048], P('section', 'dp'), may hold values from -8 to 8
- norm_gain: float32 [16, 2048], P('section'), may hold values from 0.5 to 1.5
- in_weight: float32 [16, 2, 2048, 512], P('section', None, 'dp', 'hid'), may hold values from -0.125 to 0.125
- out_weight: float32 [16, 512, 2048], P('section', 'hid', 'dp'), may hold values from -0.25 to 0.25
- in_codes: int32 [16, 2, 2048, 512], P('section', None, 'dp', 'hid'), may hold values from 0 to 32511
- out_codes: int32 [16, 512, 2048], P('section', 'hid', 'dp'), may hold values from 0 to 32511
- in_scales: float32 [16, 2, 2, 2048, 2], P('section', None, None, 'dp', 'hid'), may hold values from 0.005 to 0.05
- out_scales: float32 [16, 2, 2, 2048], P('section', None, 'hid', 'dp'), may hold values from 0.005 to 0.05
- section_lags: int32 [16], P('section'), may hold values from 1 to 4
Outputs:
- next_input: bfloat16 [16, 3072, 2048], P('section', 'dp')
- input_grad: bfloat16 [16, 3072, 2048], P('section', 'dp')
- in_update: float32 [16, 2, 2048, 512], P('section', None, 'dp', 'hid')
- out_update: float32 [16, 512, 2048], P('section', 'hid', 'dp')
The draws below stay inside these ranges and needn't reach their ends.
Inputs may be any that keep to these rules, and one draw needn't show every extreme that they name: `in_codes`: each code holds a first-moment code of 0 to 126 times 256 plus a second-moment code of 0 to 255. `out_codes`: each code holds a first-moment code of 0 to 126 times 256 plus a second-moment code of 0 to 255.
All inputs are finite; a program needn't handle non-finite values.
Results may differ from the reference program's by a relative error of at most 0.012.
Values may be sent and summed in bfloat16 or wider, within the bound.
No kernel may reach another device: no remote copies, remote signals or barrier semaphores. Data moves between devices by JAX's collectives and lax.ppermute only.
A program may use at most 64 MiB of HBM per device.

```python
import math
import jax
import jax.numpy as jnp
from jax import lax

D = 2048
FF = 512
ROWS = 192
QB = 256
STEP = 1000
SECTIONS = 16
ROWS_ALL = 3072
N_HID = 2


def set_ends(values, stream_key, low, top_value):
    extent = values.shape
    spot = [jax.random.randint(jax.random.fold_in(stream_key, axis), (), 0, extent[axis]) for axis in range(len(extent))]
    values = values.at[tuple(spot)].set(low)
    longest = extent.index(max(extent))
    spot[longest] = (spot[longest] + 1) % extent[longest]
    return values.at[tuple(spot)].set(top_value)


def raised(entries, rng, source, target, blocks, factor):
    def block_of(dim):
        return (jnp.arange(entries.shape[dim]) // (entries.shape[dim] // blocks)).reshape((-1,) + (1,) * (entries.ndim - 1 - dim))

    one_side = jax.random.permutation(rng, blocks)[block_of(target)]
    far = (block_of(target) + blocks // 2) % blocks
    return jnp.where((block_of(source) == one_side) | (block_of(source) == far), factor * entries, entries)


def shard_levels(own_key, dims, pieces, least, largest):
    factor_of = 1.0
    for position, blocks in pieces:
        steps = jax.random.uniform(jax.random.fold_in(jax.random.fold_in(own_key, 6), position), (blocks,), jnp.float32, least / len(pieces), largest / len(pieces))
        factor_of = factor_of * jnp.repeat(jnp.exp(steps), dims[position] // blocks).reshape((-1,) + (1,) * (len(dims) - 1 - position))
    return factor_of


def scatter_about(stream_key, shape, deviation, reach, shards=(), held_as=jnp.bfloat16):
    array = jax.random.normal(stream_key, shape, jnp.float32) * deviation
    if len(shards) > 0:
        array = shard_levels(stream_key, shape, shards, -0.22, 0.18) * array
    return jnp.clip(array, min=-reach, max=reach).astype(held_as)


def noise_with(key, dims, width, most, shards, heavy, dtype=jnp.bfloat16):
    array = width * jax.random.normal(key, dims, jnp.float32)
    if shards:
        array = array * shard_levels(key, dims, shards, -0.22, 0.18)
    return jnp.clip(raised(array, jax.random.fold_in(key, 3), *heavy), -most, most).astype(dtype)


def setup_inputs(seed: int = 0) -> dict:
    key_of = jax.random.split(jax.random.key(seed), 12)
    return {
        "forward_input": scatter_about(key_of[0], (SECTIONS, ROWS_ALL, D), 1.0, 6.0, ((0, 16), (1, 16))),
        "backward_input": scatter_about(key_of[1], (SECTIONS, ROWS_ALL, D), 1.0, 6.0, ((0, 16), (1, 16))),
        "output_grad": noise_with(key_of[2], (SECTIONS, ROWS_ALL, D), 1.0, 8.0, ((0, 16), (1, 16)), (1, 2, 16, 2.0)),
        "norm_gain": jnp.clip(1.0 + 0.1 * jax.random.normal(key_of[3], (SECTIONS, D), jnp.float32), 0.5, 1.5),
        "in_weight": scatter_about(key_of[4], (SECTIONS, 2, D, FF), D ** -0.5, 0.125, ((0, 16), (2, 16), (3, 2)), jnp.float32),
        "out_weight": scatter_about(key_of[5], (SECTIONS, FF, D), FF ** -0.5, 0.25, ((0, 16), (1, 2), (2, 16)), jnp.float32),
        "in_codes": set_ends(jax.random.randint(key_of[6], (SECTIONS, 2, D, FF), 0, 32512), jax.random.fold_in(key_of[6], 1), 0, 32511).astype(jnp.int32),
        "out_codes": set_ends(jax.random.randint(key_of[7], (SECTIONS, FF, D), 0, 32512), jax.random.fold_in(key_of[7], 1), 0, 32511).astype(jnp.int32),
        "in_scales": jnp.clip(jnp.exp(math.log(0.05) - 2.3025851 * jax.random.uniform(key_of[8], (SECTIONS, 2, 2, D, FF // QB), jnp.float32) ** shard_levels(key_of[8], (SECTIONS, 2, 2, D, FF // QB), ((0, 16), (3, 16), (4, 2)), -0.2, 0.2)), 0.005, 0.05),
        "out_scales": jnp.clip(jnp.exp(math.log(0.05) - 2.3025851 * jax.random.uniform(key_of[9], (SECTIONS, 2, FF // QB, D), jnp.float32) ** shard_levels(key_of[9], (SECTIONS, 2, FF // QB, D), ((0, 16), (2, 2), (3, 16)), -0.2, 0.2)), 0.005, 0.05),
        "section_lags": set_ends(jax.random.randint(key_of[10], (SECTIONS,), 1, 5), jax.random.fold_in(key_of[10], 1), 1, 4).astype(jnp.int32),
    }


BETA_ONE = 0.9
BETA_TWO = 0.999
ADAM_EPS = 1e-08
NORM_EPS = 1e-06
LEARN_RATE = 0.003

def dequant(codes, first_scale, second_scale):
    high = (codes // 256).astype(jnp.float32)
    low = (codes % 256).astype(jnp.float32)
    moment_m = first_scale * (high - 63.0) / 63.0
    moment_v = jnp.square(second_scale * (0.25 + 0.75 * low / 255.0))
    return (moment_m, moment_v)

def direction(moment_m, moment_v, count):
    return moment_m / (1.0 - BETA_ONE ** count) / (jnp.sqrt(moment_v / (1.0 - BETA_TWO ** count)) + ADAM_EPS)

def normalize(inputs, gain):
    values = inputs.astype(jnp.float32)
    factor = lax.rsqrt(lax.optimization_barrier(jnp.mean(values * values, axis=-1, keepdims=True)) + NORM_EPS)
    return ((values * factor * gain).astype(jnp.bfloat16), factor, values)

def one_section(items):
    fwd_rows, bwd_rows, out_cot, gain, w_in, w_out, c_in, c_out, s_in, s_out, lag_count = items
    lag_value = lag_count.astype(jnp.float32)
    m_in, v_in = dequant(c_in, jnp.repeat(s_in[0], QB, axis=-1), jnp.repeat(s_in[1], QB, axis=-1))
    m_out, v_out = dequant(c_out, jnp.repeat(s_out[0], QB, axis=0), jnp.repeat(s_out[1], QB, axis=0))
    pred_in = (w_in - LEARN_RATE * lag_value * direction(m_in, v_in, STEP - 1)).astype(jnp.bfloat16)
    pred_out = (w_out - LEARN_RATE * lag_value * direction(m_out, v_out, STEP - 1)).astype(jnp.bfloat16)
    rows_all = fwd_rows.shape[0]
    half_ff = FF // N_HID
    hp = lax.Precision.HIGHEST
    normed, factor, values = normalize(fwd_rows, gain)
    gate_val = jnp.dot(normed, pred_in[0], preferred_element_type=jnp.float32)
    up_val = jnp.dot(normed, pred_in[1], preferred_element_type=jnp.float32)
    hidden = (gate_val * jax.nn.sigmoid(gate_val) * up_val).astype(jnp.bfloat16)
    parts = jnp.einsum('rkf,kfd->krd', hidden.reshape(rows_all, N_HID, half_ff).astype(jnp.float32), pred_out.reshape(N_HID, half_ff, D).astype(jnp.float32), precision=hp)
    summed = lax.optimization_barrier(jnp.sum(parts.astype(jnp.bfloat16).astype(jnp.float32), axis=0))
    ahead = (values + summed).astype(jnp.bfloat16)
    normed_b, factor_b, values_b = normalize(bwd_rows, gain)
    gate_b = jnp.dot(normed_b, pred_in[0], preferred_element_type=jnp.float32)
    up_b = jnp.dot(normed_b, pred_in[1], preferred_element_type=jnp.float32)
    sig_b = jax.nn.sigmoid(gate_b)
    hidden_b = (gate_b * sig_b * up_b).astype(jnp.bfloat16)
    grad_h = jnp.dot(out_cot, pred_out.T, preferred_element_type=jnp.float32)
    grad_gate = (grad_h * up_b * sig_b * (1.0 + gate_b * (1.0 - sig_b))).astype(jnp.bfloat16)
    grad_up = (grad_h * gate_b * sig_b).astype(jnp.bfloat16)
    gate_parts = jnp.einsum('rkf,dkf->krd', grad_gate.reshape(rows_all, N_HID, half_ff).astype(jnp.float32), pred_in[0].reshape(D, N_HID, half_ff).astype(jnp.float32), precision=hp)
    up_parts = jnp.einsum('rkf,dkf->krd', grad_up.reshape(rows_all, N_HID, half_ff).astype(jnp.float32), pred_in[1].reshape(D, N_HID, half_ff).astype(jnp.float32), precision=hp)
    grad_n = lax.optimization_barrier(jnp.sum((gate_parts + up_parts).astype(jnp.bfloat16).astype(jnp.float32), axis=0))
    scaled = gain * grad_n
    grad_x = out_cot.astype(jnp.float32) + factor_b * scaled - values_b * factor_b ** 3 * lax.optimization_barrier(jnp.mean(scaled * values_b, axis=-1, keepdims=True))
    back_rows = grad_x.astype(jnp.bfloat16)
    groups = rows_all // ROWS
    n_grp = normed_b.reshape(groups, ROWS, D).astype(jnp.float32)
    g_grp = grad_gate.reshape(groups, ROWS, FF).astype(jnp.float32)
    u_grp = grad_up.reshape(groups, ROWS, FF).astype(jnp.float32)
    h_grp = hidden_b.reshape(groups, ROWS, FF).astype(jnp.float32)
    y_grp = out_cot.reshape(groups, ROWS, D).astype(jnp.float32)

    def group_sum(left, right, form):
        terms = jnp.einsum(form, left, right, precision=hp)
        return lax.optimization_barrier(jnp.sum(terms.astype(jnp.bfloat16).astype(jnp.float32), axis=0)) / rows_all
    grad_in = jnp.stack([group_sum(n_grp, g_grp, 'srd,srf->sdf'), group_sum(n_grp, u_grp, 'srd,srf->sdf')])
    grad_out = group_sum(h_grp, y_grp, 'srf,srd->sfd')
    new_m_in = BETA_ONE * m_in + (1.0 - BETA_ONE) * grad_in
    new_v_in = BETA_TWO * v_in + (1.0 - BETA_TWO) * grad_in * grad_in
    new_m_out = BETA_ONE * m_out + (1.0 - BETA_ONE) * grad_out
    new_v_out = BETA_TWO * v_out + (1.0 - BETA_TWO) * grad_out * grad_out
    return (ahead, back_rows, direction(new_m_in, new_v_in, STEP), direction(new_m_out, new_v_out, STEP))

def reference(forward_input, backward_input, output_grad, norm_gain, in_weight, out_weight, in_codes, out_codes, in_scales, out_scales, section_lags):
    ahead, back_rows, in_update, out_update = lax.map(one_section, (forward_input, backward_input, output_grad, norm_gain, in_weight, out_weight, in_codes, out_codes, in_scales, out_scales, section_lags))
    zero_rows = jnp.zeros_like(ahead[:1])
    next_input = jnp.concatenate([zero_rows, ahead[:-1]], axis=0)
    input_grad = jnp.concatenate([back_rows[1:], zero_rows], axis=0)
    return (next_input, input_grad, in_update, out_update)
```

```python
import functools

import jax
import jax.numpy as jnp
from jax import lax
from jax.experimental import pallas as pl
from jax.experimental.pallas import tpu as pltpu
from jax.sharding import Mesh
from jax.sharding import PartitionSpec as P

STEP = 1000
DP = ("y", "xh")
BETA_ONE = 0.9
BETA_TWO = 0.999
ADAM_EPS = 1e-08
NORM_EPS = 1e-06
LEARN_RATE = 0.003

F32 = jnp.float32
BF16 = jnp.bfloat16
VM = pl.BlockSpec(memory_space=pltpu.VMEM)
SM = pl.BlockSpec(memory_space=pltpu.SMEM)
NT = (((1,), (1,)), ((), ()))


def call(body, out, args, scratch=(), flops=0, n_smem=0, name=None):
    moved = sum(a.size * a.dtype.itemsize for a in (*args, *out))
    return pl.pallas_call(
        body,
        out_shape=tuple(jax.ShapeDtypeStruct(o.shape, o.dtype) for o in out),
        in_specs=[SM] * n_smem + [VM] * (len(args) - n_smem),
        out_specs=tuple(VM for _ in out),
        scratch_shapes=list(scratch),
        cost_estimate=pl.CostEstimate(flops=flops, bytes_accessed=moved, transcendentals=0),
        name=name,
    )(*args)


def struct(shape, dtype=BF16):
    return jax.ShapeDtypeStruct(shape, dtype)


def column(row, n):
    return jnp.broadcast_to(row, (n, row.shape[1])).T


def moments(codes, scale_m, scale_v):
    high = (codes >> 8).astype(F32)
    low = (codes & 255).astype(F32)
    return scale_m * (high - 63.0) / 63.0, scale_v * (0.25 + 0.75 * low / 255.0)


def predicted(weight, codes, scale_m, scale_v, rate):
    m, root = moments(codes, scale_m, scale_v)
    c1 = 1.0 - BETA_ONE ** (STEP - 1)
    c2 = (1.0 - BETA_TWO ** (STEP - 1)) ** 0.5
    return weight - rate * (m / c1 / (root / c2 + ADAM_EPS))


def predict_body(lag_ref, w_in, c_in, s_in, w_out, c_out, s_out, send):
    rate = LEARN_RATE * lag_ref[0].astype(F32)
    parts = []
    for i in range(2):
        sm = column(s_in[i : i + 1, :], 128)
        sv = column(s_in[2 + i : 3 + i, :], 128)
        parts.append([
            predicted(w_in[i, :, h * 128 : h * 128 + 128], c_in[i, :, h * 128 : h * 128 + 128], sm, sv, rate)
            for h in range(2)
        ])
    down = []
    for h in range(2):
        rows = slice(h * 128, h * 128 + 128)
        down.append(predicted(w_out[rows, :], c_out[rows, :], s_out[0:1, :], s_out[1:2, :], rate).T)
    parts.append(down)
    for i in range(3):
        for h in range(2):
            piece = parts[i][h].astype(BF16)
            for j in range(8):
                send[2 * j + h, :, i * 128 : i * 128 + 128] = piece


def rms(x):
    return lax.rsqrt(jnp.mean(x * x, axis=-1, keepdims=True) + NORM_EPS)


def gather_body(normed_arrays, k_ref, gain_ref, *refs):
    n = len(normed_arrays)
    ins, outs = refs[: 3 * n], refs[3 * n :]
    k = k_ref[0]
    gain = gain_ref[...]
    for a, norm in enumerate(normed_arrays):
        own, near, far = ins[3 * a : 3 * a + 3]
        out = outs[a]

        def step(i, carry, own=own, near=near, far=far, out=out, norm=norm):
            r = pl.multiple_of(i * 16, 16)
            rk = pl.multiple_of(k * 96 + i * 16, 16)
            rm = pl.multiple_of((1 - k) * 96 + i * 16, 16)
            for b, v in enumerate((own[pl.ds(rk, 16), :], own[pl.ds(rm, 16), :], near[pl.ds(r, 16), :], far[pl.ds(r, 16), :])):
                if norm:
                    x = v.astype(F32)
                    v = (x * rms(x) * gain).astype(BF16)
                out[pl.ds(pl.multiple_of(b * 96 + i * 16, 16), 16), :] = v
            return carry

        lax.fori_loop(0, 6, step, 0)


def backward_body(nb, dy, w, grads, dgu, gu_acc, dh_acc, left):
    gu_acc[...] = jnp.zeros_like(gu_acc)
    dh_acc[...] = jnp.zeros_like(dh_acc)

    def contract(j, carry):
        d = pl.ds(pl.multiple_of(j * 512, 512), 512)
        gu_acc[...] += jnp.dot(nb[:, d], w[d, 0:256], preferred_element_type=F32)
        dh_acc[...] += jnp.dot(dy[:, d], w[d, 256:384], preferred_element_type=F32)
        return carry

    lax.fori_loop(0, 4, contract, 0)
    for b in range(3):
        rows = slice(b * 128, b * 128 + 128)
        g, u, dh = gu_acc[rows, 0:128], gu_acc[rows, 128:256], dh_acc[rows, :]
        s = jax.nn.sigmoid(g)
        gs = g * s
        dg = dh * u * s * (1.0 + g * (1.0 - s))
        du = dh * gs
        dgu[rows, 0:128] = dg.astype(BF16)
        dgu[rows, 128:256] = du.astype(BF16)
        left[0:128, rows] = dg.T.astype(BF16)
        left[128:256, rows] = du.T.astype(BF16)
        left[256:384, rows] = (gs * u).T.astype(BF16)

    def expand(j, carry):
        d = pl.ds(pl.multiple_of(j * 256, 256), 256)
        a = jnp.dot(left[0:256, :], nb[:, d], preferred_element_type=F32).astype(BF16)
        b = jnp.dot(left[256:384, :], dy[:, d], preferred_element_type=F32).astype(BF16)
        for h in range(2):
            lanes = slice(h * 128, h * 128 + 128)
            grads[2 * j + h, 0:256, :] = a[:, lanes]
            grads[2 * j + h, 256:384, :] = b[:, lanes]
        return carry

    lax.fori_loop(0, 8, expand, 0)


def project(left, w, first, last, keep, send):
    def step(j, carry):
        d = pl.ds(pl.multiple_of(j * 256, 256), 256)
        r = lax.dot_general(left[...], w[d, first:last], NT, preferred_element_type=F32).astype(BF16)
        keep[0:96, d] = r[0:96]
        send[0:96, d] = r[96:192]
        keep[96:192, d] = r[192:288]
        send[96:192, d] = r[288:384]
        return carry

    lax.fori_loop(0, 8, step, 0)


def cotangent_body(dgu, w, keep, send):
    project(dgu, w, 0, 256, keep, send)


def forward_body(nf, w, keep, send, gu_acc, hidden):
    gu_acc[...] = jnp.zeros_like(gu_acc)

    def contract(j, carry):
        d = pl.ds(pl.multiple_of(j * 512, 512), 512)
        gu_acc[...] += jnp.dot(nf[:, d], w[d, 0:256], preferred_element_type=F32)
        return carry

    lax.fori_loop(0, 4, contract, 0)
    for b in range(3):
        rows = slice(b * 128, b * 128 + 128)
        g, u = gu_acc[rows, 0:128], gu_acc[rows, 128:256]
        hidden[rows, :] = (g * jax.nn.sigmoid(g) * u).astype(BF16)
    project(hidden, w, 256, 384, keep, send)


def pair_body(keep, recv, out):
    out[...] = (keep[96:192, :].astype(F32) + recv[96:192, :].astype(F32)).astype(BF16)


def total(keep, recv, other, rows):
    return keep[rows, :].astype(F32) + recv[rows, :].astype(F32) + other[rows, :].astype(F32)


def ahead_body(k_ref, x, keep, recv, other, out):
    k = k_ref[0]

    def step(i, carry):
        rows = pl.ds(pl.multiple_of(i * 16, 16), 16)
        mine = pl.ds(pl.multiple_of(k * 96 + i * 16, 16), 16)
        out[rows, :] = (x[mine, :].astype(F32) + total(keep, recv, other, rows)).astype(BF16)
        return carry

    lax.fori_loop(0, 6, step, 0)


def back_body(k_ref, gain_ref, x_ref, dy, keep, recv, other, out):
    k = k_ref[0]
    gain = gain_ref[...]

    def step(i, carry):
        rows = pl.ds(pl.multiple_of(i * 16, 16), 16)
        mine = pl.ds(pl.multiple_of(k * 96 + i * 16, 16), 16)
        x = x_ref[mine, :].astype(F32)
        r = rms(x)
        a = gain * total(keep, recv, other, rows)
        dot = jnp.mean(a * x, axis=-1, keepdims=True)
        out[rows, :] = (dy[mine, :].astype(F32) + r * a - x * (r * r * r * dot)).astype(BF16)
        return carry

    lax.fori_loop(0, 6, step, 0)


def stepped(m, root, grad):
    m2 = BETA_ONE * m + (1.0 - BETA_ONE) * grad
    v2 = BETA_TWO * (root * root) + (1.0 - BETA_TWO) * grad * grad
    return m2 / (1.0 - BETA_ONE**STEP) / (jnp.sqrt(v2 / (1.0 - BETA_TWO**STEP)) + ADAM_EPS)


def update_body(rows_all, recv, c_in, s_in, c_out, s_out, in_update, out_update):
    def summed(h, rows):
        acc = recv[h, rows, :].astype(F32)
        for j in range(1, 8):
            acc = acc + recv[2 * j + h, rows, :].astype(F32)
        return acc / rows_all

    for i in range(2):
        sm = column(s_in[i : i + 1, :], 128)
        sv = column(s_in[2 + i : 3 + i, :], 128)
        for h in range(2):
            lanes = slice(h * 128, h * 128 + 128)
            m, root = moments(c_in[i, :, lanes], sm, sv)
            in_update[i, :, lanes] = stepped(m, root, summed(h, slice(i * 128, i * 128 + 128)).T)
    for h in range(2):
        rows = slice(h * 128, h * 128 + 128)
        m, root = moments(c_out[rows, :], s_out[0:1, :], s_out[1:2, :])
        out_update[rows, :] = stepped(m, root, summed(h, slice(256, 384)))


def local(fwd, bwd, cot, gain, w_in, w_out, c_in, c_out, s_in, s_out, lags):
    x_f, x_b, dy = fwd[0], bwd[0], cot[0]
    c_in, c_out = c_in[0], c_out[0]
    s_in, s_out = s_in.reshape(4, 128), s_out.reshape(2, 128)
    k = lax.axis_index("hid")
    k_arr = k.astype(jnp.int32).reshape(1)
    swap = [(0, 1), (1, 0)]
    sections = lax.axis_size("section")

    def half(x):
        return lax.dynamic_slice_in_dim(x, k * 96, 96, 0)

    def across(x):
        return lax.ppermute(x, "xh", swap)

    def on_chip(x):
        return lax.ppermute(x, "hid", swap)

    def exchange(x):
        return lax.all_to_all(x, DP, 0, 0, tiled=True)

    (send,) = call(
        predict_body, [struct((16, 128, 384))],
        [lags, w_in[0], c_in, s_in, w_out[0], c_out, s_out], n_smem=1, name="predict",
    )
    weights = exchange(send).reshape(2048, 384)

    near_b, near_y, near_f = across(half(x_b)), across(half(dy)), across(half(x_f))
    far_b, far_y, far_f = on_chip(near_b), on_chip(near_y), on_chip(near_f)
    tokens = struct((384, 2048))
    nb, dyc = call(
        functools.partial(gather_body, (True, False)), [tokens, tokens],
        [k_arr, gain, x_b, near_b, far_b, dy, near_y, far_y], n_smem=1, name="gather_b",
    )
    (nf,) = call(
        functools.partial(gather_body, (True,)), [tokens],
        [k_arr, gain, x_f, near_f, far_f], n_smem=1, name="gather_f",
    )

    grads, dgu = call(
        backward_body, [struct((16, 384, 128)), struct((384, 256))], [nb, dyc, weights],
        scratch=[pltpu.VMEM((384, 256), F32), pltpu.VMEM((384, 128), F32), pltpu.VMEM((384, 384), BF16)],
        flops=4 * 384 * 384 * 2048, name="backward",
    )
    received = exchange(grads)

    part = struct((192, 2048))
    piece = struct((96, 2048))
    e_keep, e_send = call(cotangent_body, [part, part], [dgu, weights], flops=2 * 384 * 256 * 2048, name="cotangent")
    e_recv = on_chip(e_send)
    (e_pair,) = call(pair_body, [piece], [e_keep, e_recv], name="pair_e")
    e_other = across(e_pair)
    (back,) = call(back_body, [piece], [k_arr, gain, x_b, dy, e_keep, e_recv, e_other], n_smem=1, name="back")

    q_keep, q_send = call(
        forward_body, [part, part], [nf, weights],
        scratch=[pltpu.VMEM((384, 256), F32), pltpu.VMEM((384, 128), BF16)],
        flops=2 * 384 * 384 * 2048, name="forward",
    )
    q_recv = on_chip(q_send)
    (q_pair,) = call(pair_body, [piece], [q_keep, q_recv], name="pair_q")
    q_other = across(q_pair)
    (ahead,) = call(ahead_body, [piece], [k_arr, x_f, q_keep, q_recv, q_other], n_smem=1, name="ahead")

    def relay(x, distance):
        moves = [(s, s + distance) for s in range(sections) if 0 <= s + distance < sections]
        same = [(2 * s + h, 2 * t + h) for s, t in moves for h in range(2)]
        cross = [(2 * s + h, 2 * t + 1 - h) for s, t in moves for h in range(2)]
        axes = ("section", "hid")
        a, b = lax.ppermute(x, axes, same), lax.ppermute(x, axes, cross)
        first = jnp.where(k == 0, a, b)
        second = jnp.where(k == 0, b, a)
        return jnp.concatenate([first, second], axis=0)

    back_rows = relay(back, -1)
    next_rows = relay(ahead, 1)

    rows_all = dy.shape[0] * lax.axis_size(DP)
    in_update, out_update = call(
        functools.partial(update_body, float(rows_all)),
        [struct((2, 128, 256), F32), struct((256, 128), F32)],
        [received, c_in, s_in, c_out, s_out], name="update",
    )
    return next_rows[None], back_rows[None], in_update[None], out_update[None]


def solution(mesh):
    split = Mesh(
        mesh.devices.reshape(mesh.shape["section"], 8, 2, mesh.shape["hid"]),
        ("section", "y", "xh", "hid"),
    )
    return jax.shard_map(
        local,
        mesh=split,
        in_specs=(
            P("section", DP, None),
            P("section", DP, None),
            P("section", DP, None),
            P("section", None),
            P("section", None, DP, "hid"),
            P("section", "hid", DP),
            P("section", None, DP, "hid"),
            P("section", "hid", DP),
            P("section", None, None, DP, "hid"),
            P("section", None, "hid", DP),
            P("section"),
        ),
        out_specs=(
            P("section", DP, None),
            P("section", DP, None),
            P("section", None, DP, "hid"),
            P("section", "hid", DP),
        ),
        check_vma=False,
    )
```

```python
import functools

import jax
import jax.numpy as jnp
from jax import lax
from jax.experimental import pallas as pl
from jax.experimental.pallas import tpu as pltpu
from jax.sharding import Mesh
from jax.sharding import PartitionSpec as P

STEP = 1000
DP = ("y", "xh")
BETA_ONE = 0.9
BETA_TWO = 0.999
ADAM_EPS = 1e-08
NORM_EPS = 1e-06
LEARN_RATE = 0.003

F32 = jnp.float32
BF16 = jnp.bfloat16
VM = pl.BlockSpec(memory_space=pltpu.VMEM)
HB = pl.BlockSpec(memory_space=pltpu.HBM)
SM = pl.BlockSpec(memory_space=pltpu.SMEM)
NT = (((1,), (1,)), ((), ()))


def call(body, out, args, scratch=(), flops=0, n_smem=0, hbm_in=(), hbm_out=(), alias=None):
    moved = sum(a.size * a.dtype.itemsize for a in (*args, *out))
    args = [pltpu.with_memory_space_constraint(a, pltpu.HBM) if i in hbm_in else a for i, a in enumerate(args)]
    specs = [HB if i in hbm_in else SM if i < n_smem else VM for i in range(len(args))]
    return pl.pallas_call(
        body,
        out_shape=tuple((pltpu.HBM if i in hbm_out else jax.ShapeDtypeStruct)(o.shape, o.dtype) for i, o in enumerate(out)),
        in_specs=specs,
        out_specs=tuple(HB if i in hbm_out else VM for i in range(len(out))),
        scratch_shapes=list(scratch),
        input_output_aliases=alias or {},
        compiler_params=pltpu.CompilerParams(vmem_limit_bytes=20 * 2**20),
        cost_estimate=pl.CostEstimate(flops=flops, bytes_accessed=moved, transcendentals=0),
    )(*args)


def struct(shape, dtype=BF16):
    return jax.ShapeDtypeStruct(shape, dtype)


def column(row, n):
    return jnp.broadcast_to(row, (n, row.shape[1])).T


def moments(codes, scale_m, scale_v):
    high = (codes >> 8).astype(F32)
    low = (codes & 255).astype(F32)
    return scale_m * (high - 63.0) / 63.0, scale_v * (0.25 + 0.75 * low / 255.0)


def predicted(weight, codes, scale_m, scale_v, rate):
    m, root = moments(codes, scale_m, scale_v)
    c1 = 1.0 - BETA_ONE ** (STEP - 1)
    c2 = (1.0 - BETA_TWO ** (STEP - 1)) ** 0.5
    return weight - rate * (m / c1 / (root / c2 + ADAM_EPS))


def predict_body(lag_ref, x_ref, *refs):
    hbm, give, send = refs[:6], refs[6], refs[7]
    w_in, c_in, s_in, w_out, c_out, s_out = refs[8:14]
    blocks_ref, in_sem, out_sem = refs[14:]
    xh = x_ref[0]
    loads = [pltpu.make_async_copy(hbm[i], refs[8 + i], in_sem.at[i]) for i in range(6)]
    for load in loads:
        load.start()
    for load in loads:
        load.wait()
    rate = LEARN_RATE * lag_ref[0].astype(F32)
    sm = [column(s_in[i : i + 1, :], 128) for i in range(2)]
    sv = [column(s_in[2 + i : 3 + i, :], 128) for i in range(2)]
    for h in range(2):
        lanes = slice(h * 128, h * 128 + 128)
        for i in range(2):
            piece = predicted(w_in[i, :, lanes], c_in[i, :, lanes], sm[i], sv[i], rate)
            blocks_ref[h, :, i * 128 : i * 128 + 128] = piece.astype(BF16)
        piece = predicted(w_out[lanes, :], c_out[lanes, :], s_out[0:1, :], s_out[1:2, :], rate)
        blocks_ref[h, :, 256:384] = piece.T.astype(BF16)
    give[...] = blocks_ref[1 - xh]
    stores = [pltpu.make_async_copy(blocks_ref.at[xh], send.at[j, xh], out_sem.at[j]) for j in range(8)]
    for store in stores:
        store.start()
    for store in stores:
        store.wait()


def halves_body(k_ref, *refs):
    rows = pl.ds(pl.multiple_of(k_ref[0] * 96, 32), 96)
    loads = [pltpu.make_async_copy(refs[i].at[rows, :], refs[3 + i], refs[6].at[i]) for i in range(3)]
    for load in loads:
        load.start()
    for load in loads:
        load.wait()


def fill_body(x_ref, other, _, send, sem):
    stores = [pltpu.make_async_copy(other, send.at[j, 1 - x_ref[0]], sem.at[j]) for j in range(8)]
    for store in stores:
        store.start()
    for store in stores:
        store.wait()


def rms(x):
    return lax.rsqrt(jnp.mean(x * x, axis=-1, keepdims=True) + NORM_EPS)


def normed_hbm_body(gain_ref, own, near, far, out, rows):
    normed_body(gain_ref, own, near, far, rows)
    pltpu.sync_copy(rows, out)


def normed_body(gain_ref, own, near, far, out):
    gain = gain_ref[...]

    def step(i, carry):
        r = pl.multiple_of(i * 16, 16)
        for start, ref, at in ((0, own, r), (96, own, 96 + r), (192, near, r), (288, far, r)):
            x = ref[pl.ds(pl.multiple_of(at, 16), 16), :].astype(F32)
            out[pl.ds(pl.multiple_of(start + r, 16), 16), :] = (x * rms(x) * gain).astype(BF16)
        return carry

    lax.fori_loop(0, 6, step, 0)


def blocks(k):
    first = pl.multiple_of(96 * k, 32)
    second = pl.multiple_of(96 - 96 * k, 32)
    return ((0, first), (96, second), (192, 192), (288, 288))


def backward_body(k_ref, nb_hbm, own, near, far, w, grads, dgu, gu_acc, dh_acc, left, dy, nb, ordered, out, in_sem, sem):
    chunks = [slice(j * 512, j * 512 + 512) for j in range(4)]
    nb_loads = [pltpu.make_async_copy(nb_hbm.at[:, c], nb.at[:, c], in_sem.at[3 + j]) for j, c in enumerate(chunks)]
    loads = [
        pltpu.make_async_copy(own, dy.at[0:192, :], in_sem.at[0]),
        pltpu.make_async_copy(near, dy.at[192:288, :], in_sem.at[1]),
        pltpu.make_async_copy(far, dy.at[288:384, :], in_sem.at[2]),
    ]
    for load in nb_loads + loads:
        load.start()
    gu_acc[...] = jnp.zeros_like(gu_acc)
    dh_acc[...] = jnp.zeros_like(dh_acc)
    for load, d in zip(nb_loads, chunks):
        load.wait()
        gu_acc[...] += jnp.dot(nb[:, d], w[d, 0:256], preferred_element_type=F32)
    for load in loads:
        load.wait()

    def contract_dy(j, carry):
        d = pl.ds(pl.multiple_of(j * 512, 512), 512)
        dh_acc[...] += jnp.dot(dy[:, d], w[d, 256:384], preferred_element_type=F32)
        return carry

    lax.fori_loop(0, 4, contract_dy, 0)
    for b in range(3):
        rows = slice(b * 128, b * 128 + 128)
        g, u, dh = gu_acc[rows, 0:128], gu_acc[rows, 128:256], dh_acc[rows, :]
        s = jax.nn.sigmoid(g)
        gs = g * s
        dg = dh * u * s * (1.0 + g * (1.0 - s))
        du = dh * gs
        gu_acc[rows, 0:128] = dg
        gu_acc[rows, 128:256] = du
        left[0:128, rows] = dg.T.astype(BF16)
        left[128:256, rows] = du.T.astype(BF16)
        left[256:384, rows] = (gs * u).T.astype(BF16)

    def expand(j, carry):
        d = pl.ds(pl.multiple_of(j * 256, 256), 256)
        a = jnp.dot(left[0:256, :], nb[:, d], preferred_element_type=F32).astype(BF16)
        b = jnp.dot(left[256:384, :], dy[:, d], preferred_element_type=F32).astype(BF16)
        for h in range(2):
            lanes = slice(h * 128, h * 128 + 128)
            out[2 * j + h, 0:256, :] = a[:, lanes]
            out[2 * j + h, 256:384, :] = b[:, lanes]
        pair = pl.ds(2 * j, 2)
        pltpu.make_async_copy(out.at[pair], grads.at[pair], sem.at[j]).start()
        return carry

    lax.fori_loop(0, 8, expand, 0)
    for at, start in blocks(k_ref[0]):
        ordered[at : at + 96, :] = gu_acc[pl.ds(start, 96), :].astype(BF16)
    pltpu.sync_copy(ordered, dgu)
    for j in range(8):
        pair = pl.ds(2 * j, 2)
        pltpu.make_async_copy(out.at[pair], grads.at[pair], sem.at[j]).wait()


def project(left, w, first, last, keep, send):
    def step(j, carry):
        d = pl.ds(pl.multiple_of(j * 256, 256), 256)
        r = lax.dot_general(left[...], w[d, first:last], NT, preferred_element_type=F32).astype(BF16)
        keep[0:96, d] = r[0:96]
        send[0:96, d] = r[96:192]
        keep[96:192, d] = r[192:288]
        send[96:192, d] = r[288:384]
        return carry

    lax.fori_loop(0, 8, step, 0)


def cotangent_body(dgu_hbm, w, keep, send, dgu):
    pltpu.sync_copy(dgu_hbm, dgu)
    project(dgu, w, 0, 256, keep, send)


def forward_body(k_ref, nf_hbm, w, keep, send, gu_acc, hidden, nf, sem):
    chunks = [slice(j * 512, j * 512 + 512) for j in range(4)]
    loads = [pltpu.make_async_copy(nf_hbm.at[:, c], nf.at[:, c], sem.at[j]) for j, c in enumerate(chunks)]
    for load in loads:
        load.start()
    for j, d in enumerate(chunks):
        loads[j].wait()
        part = jnp.dot(nf[:, d], w[d, 0:256], preferred_element_type=F32)
        gu_acc[...] = part if j == 0 else gu_acc[...] + part
    for at, start in blocks(k_ref[0]):
        rows = pl.ds(start, 96)
        g, u = gu_acc[rows, 0:128], gu_acc[rows, 128:256]
        hidden[at : at + 96, :] = (g * jax.nn.sigmoid(g) * u).astype(BF16)
    project(hidden, w, 256, 384, keep, send)


def total(keep, recv, start):
    rows = pl.ds(pl.multiple_of(start, 16), 16)
    return keep[rows, :].astype(F32) + recv[rows, :].astype(F32)


def ahead_body(k_ref, x, keep, recv, own_out, pair_out):
    k = k_ref[0]

    def step(i, carry):
        r = i * 16
        rows = pl.ds(pl.multiple_of(r, 16), 16)
        mine = pl.ds(pl.multiple_of(k * 96 + r, 16), 16)
        own_out[rows, :] = (x[mine, :].astype(F32) + total(keep, recv, r)).astype(BF16)
        pair_out[rows, :] = total(keep, recv, 96 + r).astype(BF16)
        return carry

    lax.fori_loop(0, 6, step, 0)


def back_body(k_ref, gain_ref, x_own, x_near, dy, keep, recv, own_out, pair_out):
    k = k_ref[0]
    gain = gain_ref[...]

    def through_norm(x, e):
        r = rms(x)
        a = gain * e
        return r * a - x * (r * r * r * jnp.mean(a * x, axis=-1, keepdims=True))

    def step(i, carry):
        r = i * 16
        rows = pl.ds(pl.multiple_of(r, 16), 16)
        mine = pl.ds(pl.multiple_of(k * 96 + r, 16), 16)
        own = through_norm(x_own[mine, :].astype(F32), total(keep, recv, r))
        own_out[rows, :] = (dy[mine, :].astype(F32) + own).astype(BF16)
        pair_out[rows, :] = through_norm(x_near[rows, :].astype(F32), total(keep, recv, 96 + r)).astype(BF16)
        return carry

    lax.fori_loop(0, 6, step, 0)


def rejoin_body(k_ref, *refs):
    pieces, outs, sem = refs[:4], refs[4:6], refs[6]
    stores = []
    for i in range(4):
        at = k_ref[0] if i % 2 == 0 else 1 - k_ref[0]
        rows = pl.ds(pl.multiple_of(at * 96, 32), 96)
        stores.append(pltpu.make_async_copy(pieces[i], outs[i // 2].at[rows, :], sem.at[i]))
    for store in stores:
        store.start()
    for store in stores:
        store.wait()


def add_body(a, b, out):
    out[...] = (a[...].astype(F32) + b[...].astype(F32)).astype(BF16)


def stepped(m, root, grad):
    m2 = BETA_ONE * m + (1.0 - BETA_ONE) * grad
    v2 = BETA_TWO * (root * root) + (1.0 - BETA_TWO) * grad * grad
    return m2 / (1.0 - BETA_ONE**STEP) / (jnp.sqrt(v2 / (1.0 - BETA_TWO**STEP)) + ADAM_EPS)


def sum_body(x_ref, received, own_sum, give, recv, sem):
    xh = x_ref[0]
    order = ((1 - xh, give), (xh, own_sum))
    loads = []
    for n, (d, _) in enumerate(order):
        for i in range(3):
            rows = slice(i * 128, i * 128 + 128)
            loads.append(pltpu.make_async_copy(received.at[:, d, rows, :], recv.at[:, d, rows, :], sem.at[3 * n + i]))
    for load in loads:
        load.start()
    for n, (d, out) in enumerate(order):
        for i in range(3):
            rows = slice(i * 128, i * 128 + 128)
            loads[3 * n + i].wait()
            acc = recv[0, d, rows, :].astype(F32)
            for j in range(1, 8):
                acc = acc + recv[j, d, rows, :].astype(F32)
            out[rows, :] = acc.astype(out.dtype)


def update_body(rows_all, x_ref, own_sum, other_sum, c_in, s_in, c_out, s_out, in_update, out_update):
    xh = x_ref[0]
    for h, grad in ((xh, own_sum), (1 - xh, other_sum)):
        part = pl.ds(pl.multiple_of(h * 128, 128), 128)
        for i in range(2):
            sm = column(s_in[i : i + 1, :], 128)
            sv = column(s_in[2 + i : 3 + i, :], 128)
            m, root = moments(c_in[i, :, part], sm, sv)
            g = grad[i * 128 : i * 128 + 128, :].astype(F32) / rows_all
            in_update[i, :, part] = stepped(m, root, g.T)
        m, root = moments(c_out[part, :], s_out[0:1, :], s_out[1:2, :])
        out_update[part, :] = stepped(m, root, grad[256:384, :].astype(F32) / rows_all)


def tick(fwd, bwd, cot, gain, w_in, w_out, c_in, c_out, s_in, s_out, lags):
    x_f, x_b, dy = fwd[0], bwd[0], cot[0]
    c_in, c_out = c_in[0], c_out[0]
    s_in, s_out = s_in.reshape(4, 128), s_out.reshape(2, 128)
    k = lax.axis_index("hid")
    k_arr = k.astype(jnp.int32).reshape(1)
    x_arr = lax.axis_index("xh").astype(jnp.int32).reshape(1)
    swap = [(0, 1), (1, 0)]
    sections = lax.axis_size("section")

    def across(x):
        return lax.ppermute(x, "xh", swap)

    def on_chip(x):
        return lax.ppermute(x, "hid", swap)

    def exchange(x):
        return lax.all_to_all(x, "y", 0, 0, tiled=True)

    def after(x, other):
        return lax.optimization_barrier((x, other))[0]

    tokens, part, piece = struct((384, 2048)), struct((192, 2048)), struct((96, 2048))
    quarter = struct((128, 384))
    give, mine = call(
        predict_body, [quarter, struct((8, 2, 128, 384))],
        [lags, x_arr, w_in[0], c_in, s_in, w_out[0], c_out, s_out],
        scratch=[
            pltpu.VMEM((2, 128, 256), F32), pltpu.VMEM((2, 128, 256), jnp.int32), pltpu.VMEM((4, 128), F32),
            pltpu.VMEM((256, 128), F32), pltpu.VMEM((256, 128), jnp.int32), pltpu.VMEM((2, 128), F32),
            pltpu.VMEM((2, 128, 384), BF16), pltpu.SemaphoreType.DMA((6,)), pltpu.SemaphoreType.DMA((8,)),
        ],
        n_smem=2, hbm_in=range(2, 8), hbm_out=(1,),
    )
    other = across(give)
    half_b, half_y, half_f = call(
        halves_body, [piece, piece, piece], [k_arr, after(x_b, give), dy, x_f],
        scratch=[pltpu.SemaphoreType.DMA((3,))], n_smem=1, hbm_in=(1, 2, 3),
    )
    (send,) = call(
        fill_body, [struct((8, 2, 128, 384))], [x_arr, other, mine],
        scratch=[pltpu.SemaphoreType.DMA((8,))], n_smem=1, hbm_in=(2,), hbm_out=(0,), alias={2: 0},
    )
    weights = exchange(send).reshape(2048, 384)

    near_b = across(half_b)
    near_y = across(half_y)
    far_b = on_chip(near_b)
    far_y = on_chip(near_y)
    near_f = across(half_f)
    far_f = on_chip(near_f)
    (nb,) = call(normed_hbm_body, [tokens], [gain, x_b, near_b, far_b], hbm_out=(0,), scratch=[pltpu.VMEM((384, 2048), BF16)])
    (nf,) = call(
        normed_hbm_body, [tokens], [gain, x_f, near_f, far_f],
        hbm_out=(0,), scratch=[pltpu.VMEM((384, 2048), BF16)],
    )

    grads, dgu = call(
        backward_body, [struct((16, 384, 128)), struct((384, 256))], [k_arr, nb, dy, near_y, far_y, weights],
        scratch=[
            pltpu.VMEM((384, 256), F32), pltpu.VMEM((384, 128), F32),
            pltpu.VMEM((384, 384), BF16), pltpu.VMEM((384, 2048), BF16),
            pltpu.VMEM((384, 2048), BF16), pltpu.VMEM((384, 256), BF16),
            pltpu.VMEM((16, 384, 128), BF16), pltpu.SemaphoreType.DMA((7,)), pltpu.SemaphoreType.DMA((8,)),
        ],
        flops=4 * 384 * 384 * 2048, n_smem=1, hbm_in=(1, 2, 3, 4), hbm_out=(0, 1),
    )
    received = exchange(grads.reshape(8, 2, 384, 128))
    own_sum, give = call(
        sum_body, [struct((384, 128), F32), struct((384, 128))], [x_arr, received],
        scratch=[pltpu.VMEM((8, 2, 384, 128), BF16), pltpu.SemaphoreType.DMA((6,))],
        n_smem=1, hbm_in=(1,),
    )
    other_sum = across(give)

    q_keep, q_send = call(
        forward_body, [part, part], [k_arr, after(nf, dgu), weights],
        scratch=[
            pltpu.VMEM((384, 256), F32), pltpu.VMEM((384, 128), BF16),
            pltpu.VMEM((384, 2048), BF16), pltpu.SemaphoreType.DMA((4,)),
        ],
        flops=2 * 384 * 384 * 2048, n_smem=1, hbm_in=(1,),
    )
    q_recv = on_chip(q_send)
    e_keep, e_send = call(
        cotangent_body, [part, part], [after(dgu, q_send), weights],
        scratch=[pltpu.VMEM((384, 256), BF16)], flops=2 * 384 * 256 * 2048, hbm_in=(0,),
    )
    e_recv = on_chip(e_send)
    ahead = call(ahead_body, [piece, piece], [k_arr, x_f, q_keep, q_recv], n_smem=1)
    back = call(back_body, [piece, piece], [k_arr, gain, x_b, near_b, dy, e_keep, e_recv], n_smem=1)

    def relay(pieces, distance):
        moves = [(s, s + distance) for s in range(sections) if 0 <= s + distance < sections]
        same = [(2 * s + h, 2 * t + h) for s, t in moves for h in range(2)]
        cross = [(2 * s + h, 2 * t + 1 - h) for s, t in moves for h in range(2)]
        axes = ("section", "xh")
        own, pair = lax.ppermute(pieces[0], axes, same), lax.ppermute(pieces[1], axes, cross)
        (mine,) = call(add_body, [piece], [own, pair])
        return mine, on_chip(mine)

    next_halves = relay(ahead, 1)
    back_halves = relay(back, -1)
    next_rows, back_rows = call(
        rejoin_body, [part, part], [k_arr, *next_halves, *back_halves],
        scratch=[pltpu.SemaphoreType.DMA((4,))], n_smem=1, hbm_out=(0, 1),
    )

    rows_all = dy.shape[0] * lax.axis_size(DP)
    in_update, out_update = call(
        functools.partial(update_body, float(rows_all)),
        [struct((2, 128, 256), F32), struct((256, 128), F32)],
        [x_arr, own_sum, other_sum, c_in, s_in, c_out, s_out], n_smem=1,
    )
    return next_rows[None], back_rows[None], in_update[None], out_update[None]


def solution(mesh):
    split = Mesh(
        mesh.devices.reshape(mesh.shape["section"], 8, 2, mesh.shape["hid"]),
        ("section", "y", "xh", "hid"),
    )
    return jax.shard_map(
        tick,
        mesh=split,
        in_specs=(
            P("section", DP, None),
            P("section", DP, None),
            P("section", DP, None),
            P("section", None),
            P("section", None, DP, "hid"),
            P("section", "hid", DP),
            P("section", None, DP, "hid"),
            P("section", "hid", DP),
            P("section", None, None, DP, "hid"),
            P("section", None, "hid", DP),
            P("section"),
        ),
        out_specs=(
            P("section", DP, None),
            P("section", DP, None),
            P("section", None, DP, "hid"),
            P("section", "hid", DP),
        ),
        check_vma=False,
    )
```

```python
import functools

import jax
import jax.numpy as jnp
from jax import lax
from jax.experimental import pallas as pl
from jax.experimental.pallas import tpu as pltpu
from jax.sharding import Mesh
from jax.sharding import PartitionSpec as P

STEP = 1000
DP = ("y", "xh")
BETA_ONE = 0.9
BETA_TWO = 0.999
ADAM_EPS = 1e-08
NORM_EPS = 1e-06
LEARN_RATE = 0.003

F32 = jnp.float32
BF16 = jnp.bfloat16
VM = pl.BlockSpec(memory_space=pltpu.VMEM)
HB = pl.BlockSpec(memory_space=pltpu.HBM)
SM = pl.BlockSpec(memory_space=pltpu.SMEM)
NT = (((1,), (1,)), ((), ()))


def call(body, out, args, scratch=(), flops=0, n_smem=0, hbm_in=(), hbm_out=(), alias=None):
    moved = sum(a.size * a.dtype.itemsize for a in (*args, *out))
    args = [pltpu.with_memory_space_constraint(a, pltpu.HBM) if i in hbm_in else a for i, a in enumerate(args)]
    specs = [HB if i in hbm_in else SM if i < n_smem else VM for i in range(len(args))]
    return pl.pallas_call(
        body,
        out_shape=tuple((pltpu.HBM if i in hbm_out else jax.ShapeDtypeStruct)(o.shape, o.dtype) for i, o in enumerate(out)),
        in_specs=specs,
        out_specs=tuple(HB if i in hbm_out else VM for i in range(len(out))),
        scratch_shapes=list(scratch),
        input_output_aliases=alias or {},
        compiler_params=pltpu.CompilerParams(vmem_limit_bytes=20 * 2**20),
        cost_estimate=pl.CostEstimate(flops=flops, bytes_accessed=moved, transcendentals=0),
    )(*args)


def struct(shape, dtype=BF16):
    return jax.ShapeDtypeStruct(shape, dtype)


def column(row, n):
    return jnp.broadcast_to(row, (n, row.shape[1])).T


def moments(codes, scale_m, scale_v):
    high = (codes >> 8).astype(F32)
    low = (codes & 255).astype(F32)
    return scale_m * (high - 63.0) / 63.0, scale_v * (0.25 + 0.75 * low / 255.0)


def predicted(weight, codes, scale_m, scale_v, rate):
    m, root = moments(codes, scale_m, scale_v)
    c1 = 1.0 - BETA_ONE ** (STEP - 1)
    c2 = (1.0 - BETA_TWO ** (STEP - 1)) ** 0.5
    return weight - rate * (m / c1 / (root / c2 + ADAM_EPS))


def predict_body(lag_ref, x_ref, *refs):
    hbm, give, mine = refs[:6], refs[6], refs[7]
    w_in, c_in, s_in, w_out, c_out, s_out = refs[8:14]
    in_sem = refs[14]
    xh = x_ref[0]
    loads = [pltpu.make_async_copy(hbm[i], refs[8 + i], in_sem.at[i]) for i in range(6)]
    for load in loads:
        load.start()
    for load in loads:
        load.wait()
    rate = LEARN_RATE * lag_ref[0].astype(F32)
    sm = [column(s_in[i : i + 1, :], 128) for i in range(2)]
    sv = [column(s_in[2 + i : 3 + i, :], 128) for i in range(2)]
    for h, out in ((1 - xh, give), (xh, mine)):
        part = pl.ds(pl.multiple_of(h * 128, 128), 128)
        for i in range(2):
            piece = predicted(w_in[i, :, part], c_in[i, :, part], sm[i], sv[i], rate)
            out[:, i * 128 : i * 128 + 128] = piece.astype(BF16)
        piece = predicted(w_out[part, :], c_out[part, :], s_out[0:1, :], s_out[1:2, :], rate)
        out[:, 256:384] = piece.T.astype(BF16)


def halves_body(k_ref, x_b, dy, x_f, both, half_f, sem):
    rows = pl.ds(pl.multiple_of(k_ref[0] * 96, 32), 96)
    loads = [
        pltpu.make_async_copy(x_b.at[rows, :], both.at[0:96, :], sem.at[0]),
        pltpu.make_async_copy(dy.at[rows, :], both.at[96:192, :], sem.at[1]),
        pltpu.make_async_copy(x_f.at[rows, :], half_f, sem.at[2]),
    ]
    for load in loads:
        load.start()
    for load in loads:
        load.wait()


def rms(x):
    return lax.rsqrt(jnp.mean(x * x, axis=-1, keepdims=True) + NORM_EPS)


def row_loads(parts, rows, sem, first):
    copies, at = [], 0
    for i, part in enumerate(parts):
        copies.append(pltpu.make_async_copy(part, rows.at[at : at + part.shape[0], :], sem.at[first + i]))
        at += part.shape[0]
    return copies


def norm_rows(gain_ref, rows, out):
    gain = gain_ref[...]

    def step(i, carry):
        for start in (0, 96, 192, 288):
            at = pl.ds(pl.multiple_of(start + i * 16, 16), 16)
            x = rows[at, :].astype(F32)
            out[at, :] = (x * rms(x) * gain).astype(BF16)
        return carry

    lax.fori_loop(0, 6, step, 0)


def blocks(k):
    first = pl.multiple_of(96 * k, 32)
    second = pl.multiple_of(96 - 96 * k, 32)
    return ((0, first), (96, second), (192, 192), (288, 288))


def backward_body(k_ref, gain, x_own, y_own, near, far, w, grads, dgu, gu_acc, dh_acc, left, dy, x, nb, out, in_sem, sem):
    x_loads = row_loads((x_own, near.at[0:96, :], far.at[0:96, :]), x, in_sem, 0)
    y_loads = row_loads((y_own, near.at[96:192, :], far.at[96:192, :]), dy, in_sem, 3)
    for load in x_loads + y_loads:
        load.start()
    for load in x_loads:
        load.wait()
    norm_rows(gain, x, nb)
    gu_acc[...] = jnp.zeros_like(gu_acc)
    dh_acc[...] = jnp.zeros_like(dh_acc)

    def contract(j, carry):
        d = pl.ds(pl.multiple_of(j * 512, 512), 512)
        gu_acc[...] += jnp.dot(nb[:, d], w[d, 0:256], preferred_element_type=F32)
        return carry

    lax.fori_loop(0, 4, contract, 0)
    for load in y_loads:
        load.wait()

    def contract_dy(j, carry):
        d = pl.ds(pl.multiple_of(j * 512, 512), 512)
        dh_acc[...] += jnp.dot(dy[:, d], w[d, 256:384], preferred_element_type=F32)
        return carry

    lax.fori_loop(0, 4, contract_dy, 0)
    for b in range(3):
        rows = slice(b * 128, b * 128 + 128)
        g, u, dh = gu_acc[rows, 0:128], gu_acc[rows, 128:256], dh_acc[rows, :]
        s = jax.nn.sigmoid(g)
        gs = g * s
        dg = dh * u * s * (1.0 + g * (1.0 - s))
        du = dh * gs
        gu_acc[rows, 0:128] = dg
        gu_acc[rows, 128:256] = du
        left[0:128, rows] = dg.T.astype(BF16)
        left[128:256, rows] = du.T.astype(BF16)
        left[256:384, rows] = (gs * u).T.astype(BF16)

    def expand(j, carry):
        d = pl.ds(pl.multiple_of(j * 256, 256), 256)
        a = jnp.dot(left[0:256, :], nb[:, d], preferred_element_type=F32).astype(BF16)
        b = jnp.dot(left[256:384, :], dy[:, d], preferred_element_type=F32).astype(BF16)
        for h in range(2):
            lanes = slice(h * 128, h * 128 + 128)
            out[2 * j + h, 0:256, :] = a[:, lanes]
            out[2 * j + h, 256:384, :] = b[:, lanes]
        pair = pl.ds(2 * j, 2)
        pltpu.make_async_copy(out.at[pair], grads.at[pair], sem.at[j]).start()
        return carry

    lax.fori_loop(0, 8, expand, 0)
    for at, start in blocks(k_ref[0]):
        dgu[at : at + 96, :] = gu_acc[pl.ds(start, 96), :].astype(BF16)
    for j in range(8):
        pair = pl.ds(2 * j, 2)
        pltpu.make_async_copy(out.at[pair], grads.at[pair], sem.at[j]).wait()


def project(left, w, first, last, keep, send):
    def step(j, carry):
        d = pl.ds(pl.multiple_of(j * 256, 256), 256)
        r = lax.dot_general(left[...], w[d, first:last], NT, preferred_element_type=F32).astype(BF16)
        keep[0:96, d] = r[0:96]
        send[0:96, d] = r[96:192]
        keep[96:192, d] = r[192:288]
        send[96:192, d] = r[288:384]
        return carry

    lax.fori_loop(0, 8, step, 0)


def cotangent_body(dgu, w, keep, send):
    project(dgu, w, 0, 256, keep, send)


def forward_body(k_ref, gain, x_own, near, far, w, keep, send, gu_acc, hidden, x, nf, sem):
    loads = row_loads((x_own, near, far), x, sem, 0)
    for load in loads:
        load.start()
    for load in loads:
        load.wait()
    norm_rows(gain, x, nf)
    gu_acc[...] = jnp.zeros_like(gu_acc)

    def contract(j, carry):
        d = pl.ds(pl.multiple_of(j * 512, 512), 512)
        gu_acc[...] += jnp.dot(nf[:, d], w[d, 0:256], preferred_element_type=F32)
        return carry

    lax.fori_loop(0, 4, contract, 0)
    for at, start in blocks(k_ref[0]):
        rows = pl.ds(start, 96)
        g, u = gu_acc[rows, 0:128], gu_acc[rows, 128:256]
        hidden[at : at + 96, :] = (g * jax.nn.sigmoid(g) * u).astype(BF16)
    project(hidden, w, 256, 384, keep, send)


def total(keep, recv, start):
    rows = pl.ds(pl.multiple_of(start, 16), 16)
    return keep[rows, :].astype(F32) + recv[rows, :].astype(F32)


def ahead_body(k_ref, x, keep, recv, own_out, pair_out):
    k = k_ref[0]

    def step(i, carry):
        r = i * 16
        rows = pl.ds(pl.multiple_of(r, 16), 16)
        mine = pl.ds(pl.multiple_of(k * 96 + r, 16), 16)
        own_out[rows, :] = (x[mine, :].astype(F32) + total(keep, recv, r)).astype(BF16)
        pair_out[rows, :] = total(keep, recv, 96 + r).astype(BF16)
        return carry

    lax.fori_loop(0, 6, step, 0)


def back_body(k_ref, gain_ref, x_own, x_near, dy, keep, recv, own_out, pair_out):
    k = k_ref[0]
    gain = gain_ref[...]

    def through_norm(x, e):
        r = rms(x)
        a = gain * e
        return r * a - x * (r * r * r * jnp.mean(a * x, axis=-1, keepdims=True))

    def step(i, carry):
        r = i * 16
        rows = pl.ds(pl.multiple_of(r, 16), 16)
        mine = pl.ds(pl.multiple_of(k * 96 + r, 16), 16)
        own = through_norm(x_own[mine, :].astype(F32), total(keep, recv, r))
        own_out[rows, :] = (dy[mine, :].astype(F32) + own).astype(BF16)
        pair_out[rows, :] = through_norm(x_near[rows, :].astype(F32), total(keep, recv, 96 + r)).astype(BF16)
        return carry

    lax.fori_loop(0, 6, step, 0)


def rejoin_body(k_ref, mine, other, next_rows, back_rows, sem):
    stores = []
    for i, (piece, at) in enumerate(((mine, k_ref[0]), (other, 1 - k_ref[0]))):
        rows = pl.ds(pl.multiple_of(at * 96, 32), 96)
        stores.append(pltpu.make_async_copy(piece.at[0:96, :], next_rows.at[rows, :], sem.at[2 * i]))
        stores.append(pltpu.make_async_copy(piece.at[96:192, :], back_rows.at[rows, :], sem.at[2 * i + 1]))
    for store in stores:
        store.start()
    for store in stores:
        store.wait()


def add_body(a, b, c, d, out):
    out[0:96, :] = (a[...].astype(F32) + b[...].astype(F32)).astype(BF16)
    out[96:192, :] = (c[...].astype(F32) + d[...].astype(F32)).astype(BF16)


def stepped(m, root, grad):
    m2 = BETA_ONE * m + (1.0 - BETA_ONE) * grad
    v2 = BETA_TWO * (root * root) + (1.0 - BETA_TWO) * grad * grad
    return m2 / (1.0 - BETA_ONE**STEP) / (jnp.sqrt(v2 / (1.0 - BETA_TWO**STEP)) + ADAM_EPS)


def sum_body(x_ref, received, own_sum, give, recv, sem):
    xh = x_ref[0]
    order = ((1 - xh, give), (xh, own_sum))
    loads = []
    for n, (d, _) in enumerate(order):
        for i in range(3):
            rows = slice(i * 128, i * 128 + 128)
            loads.append(pltpu.make_async_copy(received.at[:, d, rows, :], recv.at[:, d, rows, :], sem.at[3 * n + i]))
    for load in loads:
        load.start()
    for n, (d, out) in enumerate(order):
        for i in range(3):
            rows = slice(i * 128, i * 128 + 128)
            loads[3 * n + i].wait()
            acc = recv[0, d, rows, :].astype(F32)
            for j in range(1, 8):
                acc = acc + recv[j, d, rows, :].astype(F32)
            out[rows, :] = acc.astype(out.dtype)


def update_body(rows_all, x_ref, own_sum, other_sum, c_in, s_in, c_out, s_out, in_update, out_update):
    xh = x_ref[0]
    for h, grad in ((xh, own_sum), (1 - xh, other_sum)):
        part = pl.ds(pl.multiple_of(h * 128, 128), 128)
        for i in range(2):
            sm = column(s_in[i : i + 1, :], 128)
            sv = column(s_in[2 + i : 3 + i, :], 128)
            m, root = moments(c_in[i, :, part], sm, sv)
            g = grad[i * 128 : i * 128 + 128, :].astype(F32) / rows_all
            in_update[i, :, part] = stepped(m, root, g.T)
        m, root = moments(c_out[part, :], s_out[0:1, :], s_out[1:2, :])
        out_update[part, :] = stepped(m, root, grad[256:384, :].astype(F32) / rows_all)


def tick(fwd, bwd, cot, gain, w_in, w_out, c_in, c_out, s_in, s_out, lags):
    x_f, x_b, dy = fwd[0], bwd[0], cot[0]
    c_in, c_out = c_in[0], c_out[0]
    s_in, s_out = s_in.reshape(4, 128), s_out.reshape(2, 128)
    k = lax.axis_index("hid")
    k_arr = k.astype(jnp.int32).reshape(1)
    x_arr = lax.axis_index("xh").astype(jnp.int32).reshape(1)
    swap = [(0, 1), (1, 0)]
    sections = lax.axis_size("section")

    def across(x):
        return lax.ppermute(x, "xh", swap)

    def on_chip(x):
        return lax.ppermute(x, "hid", swap)

    def exchange(x, axes):
        return lax.all_to_all(x, axes, 0, 0, tiled=True)

    def after(x, other):
        return lax.optimization_barrier((x, other))[0]

    part, piece = struct((192, 2048)), struct((96, 2048))
    xh = lax.axis_index("xh")
    quarter = struct((128, 384))
    give, mine = call(
        predict_body, [quarter, quarter],
        [lags, xh.astype(jnp.int32).reshape(1), w_in[0], c_in, s_in, w_out[0], c_out, s_out],
        scratch=[
            pltpu.VMEM((2, 128, 256), F32), pltpu.VMEM((2, 128, 256), jnp.int32), pltpu.VMEM((4, 128), F32),
            pltpu.VMEM((256, 128), F32), pltpu.VMEM((256, 128), jnp.int32), pltpu.VMEM((2, 128), F32),
            pltpu.SemaphoreType.DMA((6,)),
        ],
        n_smem=2, hbm_in=range(2, 8),
    )
    other = across(give)
    rows = jnp.where(xh == 0, jnp.concatenate([mine, other]), jnp.concatenate([other, mine])).astype(jnp.float16)
    gathered = lax.all_gather(rows, "y", axis=0, tiled=True)
    half, half_f = call(
        halves_body, [part, piece], [k_arr, after(x_b, give), dy, x_f],
        scratch=[pltpu.SemaphoreType.DMA((3,))], n_smem=1, hbm_in=(1, 2, 3),
    )

    near = across(half)
    near, half_f, gathered = lax.optimization_barrier((near, half_f, gathered))
    weights = gathered.astype(BF16)
    far = on_chip(near)
    near_f = across(half_f)
    far_f = on_chip(near_f)

    grads, dgu = call(
        backward_body, [struct((16, 384, 128)), struct((384, 256))], [k_arr, gain, x_b, dy, near, far, weights],
        scratch=[
            pltpu.VMEM((384, 256), F32), pltpu.VMEM((384, 128), F32),
            pltpu.VMEM((384, 384), BF16), pltpu.VMEM((384, 2048), BF16), pltpu.VMEM((384, 2048), BF16),
            pltpu.VMEM((384, 2048), BF16),
            pltpu.VMEM((16, 384, 128), BF16), pltpu.SemaphoreType.DMA((6,)), pltpu.SemaphoreType.DMA((8,)),
        ],
        flops=4 * 384 * 384 * 2048, n_smem=1, hbm_in=(2, 3, 4, 5), hbm_out=(0,),
    )
    received = exchange(grads.reshape(8, 2, 384, 128), "y")
    own_sum, give = call(
        sum_body, [struct((384, 128), F32), struct((384, 128))], [x_arr, received],
        scratch=[pltpu.VMEM((8, 2, 384, 128), BF16), pltpu.SemaphoreType.DMA((6,))],
        n_smem=1, hbm_in=(1,),
    )
    other_sum = across(give)

    e_keep, e_send = call(cotangent_body, [part, part], [dgu, weights], flops=2 * 384 * 256 * 2048)
    e_recv = on_chip(e_send)
    q_keep, q_send = call(
        forward_body, [part, part], [k_arr, gain, x_f, near_f, after(far_f, e_send), weights],
        scratch=[
            pltpu.VMEM((384, 256), F32), pltpu.VMEM((384, 128), BF16),
            pltpu.VMEM((384, 2048), BF16), pltpu.VMEM((384, 2048), BF16), pltpu.SemaphoreType.DMA((3,)),
        ],
        flops=2 * 384 * 384 * 2048, n_smem=1, hbm_in=(2, 3, 4),
    )
    q_recv = on_chip(q_send)
    ahead = call(ahead_body, [piece, piece], [k_arr, x_f, q_keep, q_recv], n_smem=1)
    back = call(back_body, [piece, piece], [k_arr, gain, x_b, near, dy, e_keep, e_recv], n_smem=1)

    def relay(pieces, distance):
        moves = [(s, s + distance) for s in range(sections) if 0 <= s + distance < sections]
        same = [(2 * s + h, 2 * t + h) for s, t in moves for h in range(2)]
        cross = [(2 * s + h, 2 * t + 1 - h) for s, t in moves for h in range(2)]
        axes = ("section", "xh")
        return lax.ppermute(pieces[0], axes, same), lax.ppermute(pieces[1], axes, cross)

    next_parts = relay(ahead, 1)
    back_parts = relay(back, -1)
    (joined,) = call(add_body, [part], [*next_parts, *back_parts])
    next_rows, back_rows = call(
        rejoin_body, [part, part], [k_arr, joined, on_chip(joined)],
        scratch=[pltpu.SemaphoreType.DMA((4,))], n_smem=1, hbm_out=(0, 1),
    )

    rows_all = dy.shape[0] * lax.axis_size(DP)
    in_update, out_update = call(
        functools.partial(update_body, float(rows_all)),
        [struct((2, 128, 256), F32), struct((256, 128), F32)],
        [x_arr, own_sum, other_sum, c_in, s_in, c_out, s_out], n_smem=1,
    )
    return next_rows[None], back_rows[None], in_update[None], out_update[None]


def solution(mesh):
    split = Mesh(
        mesh.devices.reshape(mesh.shape["section"], 8, 2, mesh.shape["hid"]),
        ("section", "y", "xh", "hid"),
    )
    return jax.shard_map(
        tick,
        mesh=split,
        in_specs=(
            P("section", DP, None),
            P("section", DP, None),
            P("section", DP, None),
            P("section", None),
            P("section", None, DP, "hid"),
            P("section", "hid", DP),
            P("section", None, DP, "hid"),
            P("section", "hid", DP),
            P("section", None, None, DP, "hid"),
            P("section", None, "hid", DP),
            P("section"),
        ),
        out_specs=(
            P("section", DP, None),
            P("section", DP, None),
            P("section", None, DP, "hid"),
            P("section", "hid", DP),
        ),
        check_vma=False,
    )
```

```python
import functools

import jax
import jax.numpy as jnp
from jax import lax
from jax.experimental import pallas as pl
from jax.experimental.pallas import tpu as pltpu
from jax.sharding import Mesh
from jax.sharding import PartitionSpec as P

STEP = 1000
DP = ("y", "xh")
BETA_ONE = 0.9
BETA_TWO = 0.999
ADAM_EPS = 1e-08
NORM_EPS = 1e-06
LEARN_RATE = 0.003

F32 = jnp.float32
BF16 = jnp.bfloat16
VM = pl.BlockSpec(memory_space=pltpu.VMEM)
HB = pl.BlockSpec(memory_space=pltpu.HBM)
SM = pl.BlockSpec(memory_space=pltpu.SMEM)
NT = (((1,), (1,)), ((), ()))


def call(body, out, args, scratch=(), flops=0, n_smem=0, hbm_in=(), hbm_out=(), alias=None):
    moved = sum(a.size * a.dtype.itemsize for a in (*args, *out))
    args = [pltpu.with_memory_space_constraint(a, pltpu.HBM) if i in hbm_in else a for i, a in enumerate(args)]
    specs = [HB if i in hbm_in else SM if i < n_smem else VM for i in range(len(args))]
    return pl.pallas_call(
        body,
        out_shape=tuple((pltpu.HBM if i in hbm_out else jax.ShapeDtypeStruct)(o.shape, o.dtype) for i, o in enumerate(out)),
        in_specs=specs,
        out_specs=tuple(HB if i in hbm_out else VM for i in range(len(out))),
        scratch_shapes=list(scratch),
        input_output_aliases=alias or {},
        compiler_params=pltpu.CompilerParams(vmem_limit_bytes=20 * 2**20),
        cost_estimate=pl.CostEstimate(flops=flops, bytes_accessed=moved, transcendentals=0),
    )(*args)


def struct(shape, dtype=BF16):
    return jax.ShapeDtypeStruct(shape, dtype)


def column(row, n):
    return jnp.broadcast_to(row, (n, row.shape[1])).T


def moments(codes, scale_m, scale_v):
    high = (codes >> 8).astype(F32)
    low = (codes & 255).astype(F32)
    return scale_m * (high - 63.0) / 63.0, scale_v * (0.25 + 0.75 * low / 255.0)


def predicted(weight, codes, scale_m, scale_v, rate):
    m, root = moments(codes, scale_m, scale_v)
    c1 = 1.0 - BETA_ONE ** (STEP - 1)
    c2 = (1.0 - BETA_TWO ** (STEP - 1)) ** 0.5
    return weight - rate * (m / c1 / (root / c2 + ADAM_EPS))


def predict_body(lag_ref, x_ref, *refs):
    hbm, give, mine = refs[:6], refs[6], refs[7]
    w_in, c_in, s_in, w_out, c_out, s_out = refs[8:14]
    in_sem = refs[14]
    xh = x_ref[0]
    loads = [pltpu.make_async_copy(hbm[i], refs[8 + i], in_sem.at[i]) for i in range(6)]
    for load in loads:
        load.start()
    for load in loads:
        load.wait()
    rate = LEARN_RATE * lag_ref[0].astype(F32)
    sm = [column(s_in[i : i + 1, :], 128) for i in range(2)]
    sv = [column(s_in[2 + i : 3 + i, :], 128) for i in range(2)]
    for h, out in ((1 - xh, give), (xh, mine)):
        part = pl.ds(pl.multiple_of(h * 128, 128), 128)
        for i in range(2):
            piece = predicted(w_in[i, :, part], c_in[i, :, part], sm[i], sv[i], rate)
            out[:, i * 128 : i * 128 + 128] = piece.astype(BF16)
        piece = predicted(w_out[part, :], c_out[part, :], s_out[0:1, :], s_out[1:2, :], rate)
        out[:, 256:384] = piece.T.astype(BF16)


def halves_body(k_ref, x_b, dy, x_f, both, half_f, sem):
    rows = pl.ds(pl.multiple_of(k_ref[0] * 96, 32), 96)
    loads = [
        pltpu.make_async_copy(x_b.at[rows, :], both.at[0:96, :], sem.at[0]),
        pltpu.make_async_copy(dy.at[rows, :], both.at[96:192, :], sem.at[1]),
        pltpu.make_async_copy(x_f.at[rows, :], half_f, sem.at[2]),
    ]
    for load in loads:
        load.start()
    for load in loads:
        load.wait()


def rms(x):
    return lax.rsqrt(jnp.mean(x * x, axis=-1, keepdims=True) + NORM_EPS)


def row_loads(parts, rows, sem, first):
    copies, at = [], 0
    for i, part in enumerate(parts):
        copies.append(pltpu.make_async_copy(part, rows.at[at : at + part.shape[0], :], sem.at[first + i]))
        at += part.shape[0]
    return copies


def norm_rows(gain_ref, rows, out):
    gain = gain_ref[...]

    def step(i, carry):
        for start in (0, 96, 192, 288):
            at = pl.ds(pl.multiple_of(start + i * 16, 16), 16)
            x = rows[at, :].astype(F32)
            out[at, :] = (x * rms(x) * gain).astype(BF16)
        return carry

    lax.fori_loop(0, 6, step, 0)


def blocks(k):
    first = pl.multiple_of(96 * k, 32)
    second = pl.multiple_of(96 - 96 * k, 32)
    return ((0, first), (96, second), (192, 192), (288, 288))


def backward_body(k_ref, gain, x_own, y_own, near, far, w, grads, dgu, gu_acc, dh_acc, left, dy, x, nb, out, in_sem, sem):
    x_loads = row_loads((x_own, near.at[0:96, :], far.at[0:96, :]), x, in_sem, 0)
    y_loads = row_loads((y_own, near.at[96:192, :], far.at[96:192, :]), dy, in_sem, 3)
    for load in x_loads + y_loads:
        load.start()
    for load in x_loads:
        load.wait()
    norm_rows(gain, x, nb)
    gu_acc[...] = jnp.zeros_like(gu_acc)
    dh_acc[...] = jnp.zeros_like(dh_acc)

    def contract(j, carry):
        d = pl.ds(pl.multiple_of(j * 512, 512), 512)
        gu_acc[...] += jnp.dot(nb[:, d], w[d, 0:256], preferred_element_type=F32)
        return carry

    lax.fori_loop(0, 4, contract, 0)
    for load in y_loads:
        load.wait()

    def contract_dy(j, carry):
        d = pl.ds(pl.multiple_of(j * 512, 512), 512)
        dh_acc[...] += jnp.dot(dy[:, d], w[d, 256:384], preferred_element_type=F32)
        return carry

    lax.fori_loop(0, 4, contract_dy, 0)
    for b in range(3):
        rows = slice(b * 128, b * 128 + 128)
        g, u, dh = gu_acc[rows, 0:128], gu_acc[rows, 128:256], dh_acc[rows, :]
        s = jax.nn.sigmoid(g)
        gs = g * s
        dg = dh * u * s * (1.0 + g * (1.0 - s))
        du = dh * gs
        gu_acc[rows, 0:128] = dg
        gu_acc[rows, 128:256] = du
        left[0:128, rows] = dg.T.astype(BF16)
        left[128:256, rows] = du.T.astype(BF16)
        left[256:384, rows] = (gs * u).T.astype(BF16)

    def expand(j, carry):
        d = pl.ds(pl.multiple_of(j * 256, 256), 256)
        a = jnp.dot(left[0:256, :], nb[:, d], preferred_element_type=F32).astype(BF16)
        b = jnp.dot(left[256:384, :], dy[:, d], preferred_element_type=F32).astype(BF16)
        for h in range(2):
            lanes = slice(h * 128, h * 128 + 128)
            out[2 * j + h, 0:256, :] = a[:, lanes]
            out[2 * j + h, 256:384, :] = b[:, lanes]
        pair = pl.ds(2 * j, 2)
        pltpu.make_async_copy(out.at[pair], grads.at[pair], sem.at[j]).start()
        return carry

    lax.fori_loop(0, 8, expand, 0)
    for at, start in blocks(k_ref[0]):
        dgu[at : at + 96, :] = gu_acc[pl.ds(start, 96), :].astype(BF16)
    for j in range(8):
        pair = pl.ds(2 * j, 2)
        pltpu.make_async_copy(out.at[pair], grads.at[pair], sem.at[j]).wait()


def project(left, w, first, last, keep, send):
    def step(j, carry):
        d = pl.ds(pl.multiple_of(j * 256, 256), 256)
        r = lax.dot_general(left[...], w[d, first:last], NT, preferred_element_type=F32).astype(BF16)
        keep[0:96, d] = r[0:96]
        send[0:96, d] = r[96:192]
        keep[96:192, d] = r[192:288]
        send[96:192, d] = r[288:384]
        return carry

    lax.fori_loop(0, 8, step, 0)


def cotangent_body(dgu, w, keep, send):
    project(dgu, w, 0, 256, keep, send)


def forward_body(k_ref, gain, x_own, near, far, w, keep, send, gu_acc, hidden, x, nf, sem):
    loads = row_loads((x_own, near, far), x, sem, 0)
    for load in loads:
        load.start()
    for load in loads:
        load.wait()
    norm_rows(gain, x, nf)
    gu_acc[...] = jnp.zeros_like(gu_acc)

    def contract(j, carry):
        d = pl.ds(pl.multiple_of(j * 512, 512), 512)
        gu_acc[...] += jnp.dot(nf[:, d], w[d, 0:256], preferred_element_type=F32)
        return carry

    lax.fori_loop(0, 4, contract, 0)
    for at, start in blocks(k_ref[0]):
        rows = pl.ds(start, 96)
        g, u = gu_acc[rows, 0:128], gu_acc[rows, 128:256]
        hidden[at : at + 96, :] = (g * jax.nn.sigmoid(g) * u).astype(BF16)
    project(hidden, w, 256, 384, keep, send)


def total(keep, recv, start):
    rows = pl.ds(pl.multiple_of(start, 16), 16)
    return keep[rows, :].astype(F32) + recv[rows, :].astype(F32)


def ahead_body(k_ref, x, keep, recv, own_out, pair_out):
    k = k_ref[0]

    def step(i, carry):
        r = i * 16
        rows = pl.ds(pl.multiple_of(r, 16), 16)
        mine = pl.ds(pl.multiple_of(k * 96 + r, 16), 16)
        own_out[rows, :] = (x[mine, :].astype(F32) + total(keep, recv, r)).astype(BF16)
        pair_out[rows, :] = total(keep, recv, 96 + r).astype(BF16)
        return carry

    lax.fori_loop(0, 6, step, 0)


def pair_body(keep, recv, out):
    def step(i, carry):
        rows = pl.ds(pl.multiple_of(i * 16, 16), 16)
        out[rows, :] = total(keep, recv, 96 + i * 16).astype(BF16)
        return carry

    lax.fori_loop(0, 6, step, 0)


def back_body(k_ref, gain_ref, x_own, dy, keep, recv, other, out):
    k = k_ref[0]
    gain = gain_ref[...]

    def step(i, carry):
        r = i * 16
        rows = pl.ds(pl.multiple_of(r, 16), 16)
        mine = pl.ds(pl.multiple_of(k * 96 + r, 16), 16)
        x = x_own[mine, :].astype(F32)
        inv = rms(x)
        a = gain * (total(keep, recv, r) + other[rows, :].astype(F32))
        through = inv * a - x * (inv * inv * inv * jnp.mean(a * x, axis=-1, keepdims=True))
        out[rows, :] = (dy[mine, :].astype(F32) + through).astype(BF16)
        return carry

    lax.fori_loop(0, 6, step, 0)


def rejoin_body(k_ref, mine, other, next_rows, back_rows, sem):
    stores = []
    for i, (piece, at) in enumerate(((mine, k_ref[0]), (other, 1 - k_ref[0]))):
        rows = pl.ds(pl.multiple_of(at * 96, 32), 96)
        stores.append(pltpu.make_async_copy(piece.at[0:96, :], next_rows.at[rows, :], sem.at[2 * i]))
        stores.append(pltpu.make_async_copy(piece.at[96:192, :], back_rows.at[rows, :], sem.at[2 * i + 1]))
    for store in stores:
        store.start()
    for store in stores:
        store.wait()


def add_body(a, b, c, out):
    out[0:96, :] = (a[...].astype(F32) + b[...].astype(F32)).astype(BF16)
    out[96:192, :] = c[...]


def stepped(m, root, grad):
    m2 = BETA_ONE * m + (1.0 - BETA_ONE) * grad
    v2 = BETA_TWO * (root * root) + (1.0 - BETA_TWO) * grad * grad
    return m2 / (1.0 - BETA_ONE**STEP) / (jnp.sqrt(v2 / (1.0 - BETA_TWO**STEP)) + ADAM_EPS)


def sum_body(x_ref, received, own_sum, give, recv, sem):
    xh = x_ref[0]
    order = ((1 - xh, give), (xh, own_sum))
    loads = []
    for n, (d, _) in enumerate(order):
        for i in range(3):
            rows = slice(i * 128, i * 128 + 128)
            loads.append(pltpu.make_async_copy(received.at[:, d, rows, :], recv.at[:, d, rows, :], sem.at[3 * n + i]))
    for load in loads:
        load.start()
    for n, (d, out) in enumerate(order):
        for i in range(3):
            rows = slice(i * 128, i * 128 + 128)
            loads[3 * n + i].wait()
            acc = recv[0, d, rows, :].astype(F32)
            for j in range(1, 8):
                acc = acc + recv[j, d, rows, :].astype(F32)
            out[rows, :] = acc.astype(out.dtype)


def update_body(rows_all, x_ref, own_sum, other_sum, c_in, s_in, c_out, s_out, in_update, out_update):
    xh = x_ref[0]
    for h, grad in ((xh, own_sum), (1 - xh, other_sum)):
        part = pl.ds(pl.multiple_of(h * 128, 128), 128)
        for i in range(2):
            sm = column(s_in[i : i + 1, :], 128)
            sv = column(s_in[2 + i : 3 + i, :], 128)
            m, root = moments(c_in[i, :, part], sm, sv)
            g = grad[i * 128 : i * 128 + 128, :].astype(F32) / rows_all
            in_update[i, :, part] = stepped(m, root, g.T)
        m, root = moments(c_out[part, :], s_out[0:1, :], s_out[1:2, :])
        out_update[part, :] = stepped(m, root, grad[256:384, :].astype(F32) / rows_all)


def tick(fwd, bwd, cot, gain, w_in, w_out, c_in, c_out, s_in, s_out, lags):
    x_f, x_b, dy = fwd[0], bwd[0], cot[0]
    c_in, c_out = c_in[0], c_out[0]
    s_in, s_out = s_in.reshape(4, 128), s_out.reshape(2, 128)
    k = lax.axis_index("hid")
    k_arr = k.astype(jnp.int32).reshape(1)
    x_arr = lax.axis_index("xh").astype(jnp.int32).reshape(1)
    swap = [(0, 1), (1, 0)]
    sections = lax.axis_size("section")

    def across(x):
        return lax.ppermute(x, "xh", swap)

    def on_chip(x):
        return lax.ppermute(x, "hid", swap)

    def exchange(x, axes):
        return lax.all_to_all(x, axes, 0, 0, tiled=True)

    def after(x, other):
        return lax.optimization_barrier((x, other))[0]

    part, piece = struct((192, 2048)), struct((96, 2048))
    xh = lax.axis_index("xh")
    quarter = struct((128, 384))
    give, mine = call(
        predict_body, [quarter, quarter],
        [lags, xh.astype(jnp.int32).reshape(1), w_in[0], c_in, s_in, w_out[0], c_out, s_out],
        scratch=[
            pltpu.VMEM((2, 128, 256), F32), pltpu.VMEM((2, 128, 256), jnp.int32), pltpu.VMEM((4, 128), F32),
            pltpu.VMEM((256, 128), F32), pltpu.VMEM((256, 128), jnp.int32), pltpu.VMEM((2, 128), F32),
            pltpu.SemaphoreType.DMA((6,)),
        ],
        n_smem=2, hbm_in=range(2, 8),
    )
    other = across(give)
    rows = jnp.where(xh == 0, jnp.concatenate([mine, other]), jnp.concatenate([other, mine])).astype(jnp.float16)
    gathered = lax.all_gather(rows, "y", axis=0, tiled=True)
    half, half_f = call(
        halves_body, [part, piece], [k_arr, after(x_b, give), dy, x_f],
        scratch=[pltpu.SemaphoreType.DMA((3,))], n_smem=1, hbm_in=(1, 2, 3),
    )

    near = across(half)
    near, half_f, gathered = lax.optimization_barrier((near, half_f, gathered))
    weights = gathered.astype(BF16)
    far = on_chip(near)
    near_f = across(half_f)
    far_f = on_chip(near_f)

    grads, dgu = call(
        backward_body, [struct((16, 384, 128)), struct((384, 256))], [k_arr, gain, x_b, dy, near, far, weights],
        scratch=[
            pltpu.VMEM((384, 256), F32), pltpu.VMEM((384, 128), F32),
            pltpu.VMEM((384, 384), BF16), pltpu.VMEM((384, 2048), BF16), pltpu.VMEM((384, 2048), BF16),
            pltpu.VMEM((384, 2048), BF16),
            pltpu.VMEM((16, 384, 128), BF16), pltpu.SemaphoreType.DMA((6,)), pltpu.SemaphoreType.DMA((8,)),
        ],
        flops=4 * 384 * 384 * 2048, n_smem=1, hbm_in=(2, 3, 4), hbm_out=(0,),
    )
    received = exchange(grads.reshape(8, 2, 384, 128), "y")
    own_sum, give = call(
        sum_body, [struct((384, 128), F32), struct((384, 128))], [x_arr, received],
        scratch=[pltpu.VMEM((8, 2, 384, 128), BF16), pltpu.SemaphoreType.DMA((6,))],
        n_smem=1, hbm_in=(1,),
    )
    other_sum = across(give)

    e_keep, e_send = call(cotangent_body, [part, part], [dgu, weights], flops=2 * 384 * 256 * 2048)
    e_recv = on_chip(e_send)
    q_keep, q_send = call(
        forward_body, [part, part], [k_arr, gain, x_f, near_f, after(far_f, e_send), weights],
        scratch=[
            pltpu.VMEM((384, 256), F32), pltpu.VMEM((384, 128), BF16),
            pltpu.VMEM((384, 2048), BF16), pltpu.VMEM((384, 2048), BF16), pltpu.SemaphoreType.DMA((3,)),
        ],
        flops=2 * 384 * 384 * 2048, n_smem=1, hbm_in=(2,),
    )
    q_recv = on_chip(q_send)
    ahead = call(ahead_body, [piece, piece], [k_arr, x_f, q_keep, q_recv], n_smem=1)
    (e_pair,) = call(pair_body, [piece], [e_keep, e_recv])
    e_other = across(e_pair)
    (back,) = call(back_body, [piece], [k_arr, gain, x_b, dy, e_keep, e_recv, e_other], n_smem=1)

    def relay(x, distance, turn):
        moves = [(s, s + distance) for s in range(sections) if 0 <= s + distance < sections]
        axes = ("section", "xh")
        return lax.ppermute(x, axes, [(2 * s + h, 2 * t + (h ^ turn)) for s, t in moves for h in range(2)])

    next_parts = relay(ahead[0], 1, 0), relay(ahead[1], 1, 1)
    back_part = relay(back, -1, 0)
    (joined,) = call(add_body, [part], [*next_parts, back_part])
    next_rows, back_rows = call(
        rejoin_body, [part, part], [k_arr, joined, on_chip(joined)],
        scratch=[pltpu.SemaphoreType.DMA((4,))], n_smem=1, hbm_out=(0, 1),
    )

    rows_all = dy.shape[0] * lax.axis_size(DP)
    in_update, out_update = call(
        functools.partial(update_body, float(rows_all)),
        [struct((2, 128, 256), F32), struct((256, 128), F32)],
        [x_arr, own_sum, other_sum, c_in, s_in, c_out, s_out], n_smem=1,
    )
    return next_rows[None], back_rows[None], in_update[None], out_update[None]


def solution(mesh):
    split = Mesh(
        mesh.devices.reshape(mesh.shape["section"], 8, 2, mesh.shape["hid"]),
        ("section", "y", "xh", "hid"),
    )
    return jax.shard_map(
        tick,
        mesh=split,
        in_specs=(
            P("section", DP, None),
            P("section", DP, None),
            P("section", DP, None),
            P("section", None),
            P("section", None, DP, "hid"),
            P("section", "hid", DP),
            P("section", None, DP, "hid"),
            P("section", "hid", DP),
            P("section", None, None, DP, "hid"),
            P("section", None, "hid", DP),
            P("section"),
        ),
        out_specs=(
            P("section", DP, None),
            P("section", DP, None),
            P("section", None, DP, "hid"),
            P("section", "hid", DP),
        ),
        check_vma=False,
    )
```

```python
import functools

import jax
import jax.numpy as jnp
from jax import lax
from jax.experimental import pallas as pl
from jax.experimental.pallas import tpu as pltpu
from jax.sharding import Mesh
from jax.sharding import PartitionSpec as P

STEP = 1000
DP = ("y", "xh")
BETA_ONE = 0.9
BETA_TWO = 0.999
ADAM_EPS = 1e-08
NORM_EPS = 1e-06
LEARN_RATE = 0.003

F32 = jnp.float32
BF16 = jnp.bfloat16
VM = pl.BlockSpec(memory_space=pltpu.VMEM)
HB = pl.BlockSpec(memory_space=pltpu.HBM)
SM = pl.BlockSpec(memory_space=pltpu.SMEM)
NT = (((1,), (1,)), ((), ()))


def call(body, out, args, scratch=(), flops=0, n_smem=0, hbm_in=(), hbm_out=(), alias=None):
    moved = sum(a.size * a.dtype.itemsize for a in (*args, *out))
    args = [pltpu.with_memory_space_constraint(a, pltpu.HBM) if i in hbm_in else a for i, a in enumerate(args)]
    specs = [HB if i in hbm_in else SM if i < n_smem else VM for i in range(len(args))]
    return pl.pallas_call(
        body,
        out_shape=tuple((pltpu.HBM if i in hbm_out else jax.ShapeDtypeStruct)(o.shape, o.dtype) for i, o in enumerate(out)),
        in_specs=specs,
        out_specs=tuple(HB if i in hbm_out else VM for i in range(len(out))),
        scratch_shapes=list(scratch),
        input_output_aliases=alias or {},
        compiler_params=pltpu.CompilerParams(vmem_limit_bytes=20 * 2**20),
        cost_estimate=pl.CostEstimate(flops=flops, bytes_accessed=moved, transcendentals=0),
    )(*args)


def struct(shape, dtype=BF16):
    return jax.ShapeDtypeStruct(shape, dtype)


def column(row, n):
    return jnp.broadcast_to(row, (n, row.shape[1])).T


def moments(codes, scale_m, scale_v):
    high = (codes >> 8).astype(F32)
    low = (codes & 255).astype(F32)
    return scale_m * (high - 63.0) / 63.0, scale_v * (0.25 + 0.75 * low / 255.0)


def predicted(weight, codes, scale_m, scale_v, rate):
    m, root = moments(codes, scale_m, scale_v)
    c1 = 1.0 - BETA_ONE ** (STEP - 1)
    c2 = (1.0 - BETA_TWO ** (STEP - 1)) ** 0.5
    return weight - rate * (m / c1 / (root / c2 + ADAM_EPS))


def predict_body(lag_ref, x_ref, *refs):
    hbm, give, mine = refs[:6], refs[6], refs[7]
    w_in, c_in, s_in, w_out, c_out, s_out = refs[8:14]
    in_sem = refs[14]
    xh = x_ref[0]
    loads = [pltpu.make_async_copy(hbm[i], refs[8 + i], in_sem.at[i]) for i in range(6)]
    for load in loads:
        load.start()
    for load in loads:
        load.wait()
    rate = LEARN_RATE * lag_ref[0].astype(F32)
    sm = [column(s_in[i : i + 1, :], 128) for i in range(2)]
    sv = [column(s_in[2 + i : 3 + i, :], 128) for i in range(2)]
    for h, out in ((1 - xh, give), (xh, mine)):
        part = pl.ds(pl.multiple_of(h * 128, 128), 128)
        for i in range(2):
            piece = predicted(w_in[i, :, part], c_in[i, :, part], sm[i], sv[i], rate)
            out[:, i * 128 : i * 128 + 128] = piece.astype(BF16)
        piece = predicted(w_out[part, :], c_out[part, :], s_out[0:1, :], s_out[1:2, :], rate)
        out[:, 256:384] = piece.T.astype(BF16)


def halves_body(k_ref, x_b, dy, x_f, both, half_f, sem):
    rows = pl.ds(pl.multiple_of(k_ref[0] * 96, 32), 96)
    loads = [
        pltpu.make_async_copy(x_b.at[rows, :], both.at[0:96, :], sem.at[0]),
        pltpu.make_async_copy(dy.at[rows, :], both.at[96:192, :], sem.at[1]),
        pltpu.make_async_copy(x_f.at[rows, :], half_f, sem.at[2]),
    ]
    for load in loads:
        load.start()
    for load in loads:
        load.wait()


def rms(x):
    return lax.rsqrt(jnp.mean(x * x, axis=-1, keepdims=True) + NORM_EPS)


def row_loads(parts, rows, sem, first):
    copies, at = [], 0
    for i, part in enumerate(parts):
        copies.append(pltpu.make_async_copy(part, rows.at[at : at + part.shape[0], :], sem.at[first + i]))
        at += part.shape[0]
    return copies


def norm_rows(gain_ref, rows, out):
    gain = gain_ref[...]

    def step(i, carry):
        for start in (0, 96, 192, 288):
            at = pl.ds(pl.multiple_of(start + i * 16, 16), 16)
            x = rows[at, :].astype(F32)
            out[at, :] = (x * rms(x) * gain).astype(BF16)
        return carry

    lax.fori_loop(0, 6, step, 0)


def blocks(k):
    first = pl.multiple_of(96 * k, 32)
    second = pl.multiple_of(96 - 96 * k, 32)
    return ((0, first), (96, second), (192, 192), (288, 288))


def backward_body(k_ref, gain, x_own, y_own, near, far, w, grads, dgu, gu_acc, dh_acc, left, dy, x, nb, out, in_sem, sem):
    x_loads = row_loads((x_own, near.at[0:96, :], far.at[0:96, :]), x, in_sem, 0)
    y_loads = row_loads((y_own, near.at[96:192, :], far.at[96:192, :]), dy, in_sem, 3)
    for load in x_loads + y_loads:
        load.start()
    for load in x_loads:
        load.wait()
    norm_rows(gain, x, nb)
    gu_acc[...] = jnp.dot(nb[...], w[:, 0:256], preferred_element_type=F32)
    for load in y_loads:
        load.wait()

    dh_acc[...] = jnp.dot(dy[...], w[:, 256:384], preferred_element_type=F32)
    for b in range(3):
        rows = slice(b * 128, b * 128 + 128)
        g, u, dh = gu_acc[rows, 0:128], gu_acc[rows, 128:256], dh_acc[rows, :]
        s = jax.nn.sigmoid(g)
        gs = g * s
        dg = dh * u * s * (1.0 + g * (1.0 - s))
        du = dh * gs
        gu_acc[rows, 0:128] = dg
        gu_acc[rows, 128:256] = du
        left[0:128, rows] = dg.T.astype(BF16)
        left[128:256, rows] = du.T.astype(BF16)
        left[256:384, rows] = (gs * u).T.astype(BF16)

    def expand(j, carry):
        d = pl.ds(pl.multiple_of(j * 256, 256), 256)
        a = jnp.dot(left[0:256, :], nb[:, d], preferred_element_type=F32).astype(BF16)
        b = jnp.dot(left[256:384, :], dy[:, d], preferred_element_type=F32).astype(BF16)
        for h in range(2):
            lanes = slice(h * 128, h * 128 + 128)
            out[2 * j + h, 0:256, :] = a[:, lanes]
            out[2 * j + h, 256:384, :] = b[:, lanes]
        pair = pl.ds(2 * j, 2)
        pltpu.make_async_copy(out.at[pair], grads.at[pair], sem.at[j]).start()
        return carry

    lax.fori_loop(0, 8, expand, 0, unroll=4)
    for at, start in blocks(k_ref[0]):
        dgu[at : at + 96, :] = gu_acc[pl.ds(start, 96), :].astype(BF16)
    for j in range(8):
        pair = pl.ds(2 * j, 2)
        pltpu.make_async_copy(out.at[pair], grads.at[pair], sem.at[j]).wait()


def project(left, w, first, last, keep, send):
    def step(j, carry):
        d = pl.ds(pl.multiple_of(j * 256, 256), 256)
        r = lax.dot_general(left[...], w[d, first:last], NT, preferred_element_type=F32).astype(BF16)
        keep[0:96, d] = r[0:96]
        send[0:96, d] = r[96:192]
        keep[96:192, d] = r[192:288]
        send[96:192, d] = r[288:384]
        return carry

    lax.fori_loop(0, 8, step, 0, unroll=4)


def cotangent_body(dgu, w, keep, send):
    project(dgu, w, 0, 256, keep, send)


def forward_body(k_ref, gain, x_own, near, far, w, keep, send, gu_acc, hidden, x, nf, sem):
    loads = row_loads((x_own, near, far), x, sem, 0)
    for load in loads:
        load.start()
    for load in loads:
        load.wait()
    norm_rows(gain, x, nf)
    gu_acc[...] = jnp.dot(nf[...], w[:, 0:256], preferred_element_type=F32)
    for at, start in blocks(k_ref[0]):
        rows = pl.ds(start, 96)
        g, u = gu_acc[rows, 0:128], gu_acc[rows, 128:256]
        hidden[at : at + 96, :] = (g * jax.nn.sigmoid(g) * u).astype(BF16)
    project(hidden, w, 256, 384, keep, send)


def total(keep, recv, start):
    rows = pl.ds(pl.multiple_of(start, 16), 16)
    return keep[rows, :].astype(F32) + recv[rows, :].astype(F32)


def ahead_body(k_ref, x, keep, recv, own_out, pair_out):
    k = k_ref[0]

    def step(i, carry):
        r = i * 16
        rows = pl.ds(pl.multiple_of(r, 16), 16)
        mine = pl.ds(pl.multiple_of(k * 96 + r, 16), 16)
        own_out[rows, :] = (x[mine, :].astype(F32) + total(keep, recv, r)).astype(BF16)
        pair_out[rows, :] = total(keep, recv, 96 + r).astype(BF16)
        return carry

    lax.fori_loop(0, 6, step, 0)


def pair_body(keep, recv, out):
    def step(i, carry):
        rows = pl.ds(pl.multiple_of(i * 16, 16), 16)
        out[rows, :] = total(keep, recv, 96 + i * 16).astype(BF16)
        return carry

    lax.fori_loop(0, 6, step, 0)


def back_body(k_ref, gain_ref, x_own, dy, keep, recv, other, out):
    k = k_ref[0]
    gain = gain_ref[...]

    def step(i, carry):
        r = i * 16
        rows = pl.ds(pl.multiple_of(r, 16), 16)
        mine = pl.ds(pl.multiple_of(k * 96 + r, 16), 16)
        x = x_own[mine, :].astype(F32)
        inv = rms(x)
        a = gain * (total(keep, recv, r) + other[rows, :].astype(F32))
        through = inv * a - x * (inv * inv * inv * jnp.mean(a * x, axis=-1, keepdims=True))
        out[rows, :] = (dy[mine, :].astype(F32) + through).astype(BF16)
        return carry

    lax.fori_loop(0, 6, step, 0)


def rejoin_body(k_ref, mine, other, next_rows, back_rows, sem):
    stores = []
    for i, (piece, at) in enumerate(((mine, k_ref[0]), (other, 1 - k_ref[0]))):
        rows = pl.ds(pl.multiple_of(at * 96, 32), 96)
        stores.append(pltpu.make_async_copy(piece.at[0:96, :], next_rows.at[rows, :], sem.at[2 * i]))
        stores.append(pltpu.make_async_copy(piece.at[96:192, :], back_rows.at[rows, :], sem.at[2 * i + 1]))
    for store in stores:
        store.start()
    for store in stores:
        store.wait()


def add_body(a, b, c, out):
    out[0:96, :] = (a[...].astype(F32) + b[...].astype(F32)).astype(BF16)
    out[96:192, :] = c[...]


def stepped(m, root, grad):
    m2 = BETA_ONE * m + (1.0 - BETA_ONE) * grad
    v2 = BETA_TWO * (root * root) + (1.0 - BETA_TWO) * grad * grad
    return m2 / (1.0 - BETA_ONE**STEP) / (jnp.sqrt(v2 / (1.0 - BETA_TWO**STEP)) + ADAM_EPS)


def sum_body(x_ref, received, own_sum, give, recv, sem):
    xh = x_ref[0]
    order = ((1 - xh, give), (xh, own_sum))
    loads = []
    for n, (d, _) in enumerate(order):
        for i in range(3):
            rows = slice(i * 128, i * 128 + 128)
            loads.append(pltpu.make_async_copy(received.at[:, d, rows, :], recv.at[:, d, rows, :], sem.at[3 * n + i]))
    for load in loads:
        load.start()
    for n, (d, out) in enumerate(order):
        for i in range(3):
            rows = slice(i * 128, i * 128 + 128)
            loads[3 * n + i].wait()
            acc = recv[0, d, rows, :].astype(F32)
            for j in range(1, 8):
                acc = acc + recv[j, d, rows, :].astype(F32)
            out[rows, :] = acc.astype(out.dtype)


def update_body(rows_all, x_ref, own_sum, other_sum, c_in, s_in, c_out, s_out, in_update, out_update):
    xh = x_ref[0]
    for h, grad in ((xh, own_sum), (1 - xh, other_sum)):
        part = pl.ds(pl.multiple_of(h * 128, 128), 128)
        for i in range(2):
            sm = column(s_in[i : i + 1, :], 128)
            sv = column(s_in[2 + i : 3 + i, :], 128)
            m, root = moments(c_in[i, :, part], sm, sv)
            g = grad[i * 128 : i * 128 + 128, :].astype(F32) / rows_all
            in_update[i, :, part] = stepped(m, root, g.T)
        m, root = moments(c_out[part, :], s_out[0:1, :], s_out[1:2, :])
        out_update[part, :] = stepped(m, root, grad[256:384, :].astype(F32) / rows_all)


def tick(fwd, bwd, cot, gain, w_in, w_out, c_in, c_out, s_in, s_out, lags):
    x_f, x_b, dy = fwd[0], bwd[0], cot[0]
    c_in, c_out = c_in[0], c_out[0]
    s_in, s_out = s_in.reshape(4, 128), s_out.reshape(2, 128)
    k = lax.axis_index("hid")
    k_arr = k.astype(jnp.int32).reshape(1)
    x_arr = lax.axis_index("xh").astype(jnp.int32).reshape(1)
    swap = [(0, 1), (1, 0)]
    sections = lax.axis_size("section")

    def across(x):
        return lax.ppermute(x, "xh", swap)

    def on_chip(x):
        return lax.ppermute(x, "hid", swap)

    def exchange(x, axes):
        return lax.all_to_all(x, axes, 0, 0, tiled=True)

    def after(x, other):
        return lax.optimization_barrier((x, other))[0]

    part, piece = struct((192, 2048)), struct((96, 2048))
    xh = lax.axis_index("xh")
    quarter = struct((128, 384))
    give, mine = call(
        predict_body, [quarter, quarter],
        [lags, xh.astype(jnp.int32).reshape(1), w_in[0], c_in, s_in, w_out[0], c_out, s_out],
        scratch=[
            pltpu.VMEM((2, 128, 256), F32), pltpu.VMEM((2, 128, 256), jnp.int32), pltpu.VMEM((4, 128), F32),
            pltpu.VMEM((256, 128), F32), pltpu.VMEM((256, 128), jnp.int32), pltpu.VMEM((2, 128), F32),
            pltpu.SemaphoreType.DMA((6,)),
        ],
        n_smem=2, hbm_in=range(2, 8),
    )
    other = across(give)
    rows = jnp.where(xh == 0, jnp.concatenate([mine, other]), jnp.concatenate([other, mine])).astype(jnp.float16)
    gathered = lax.all_gather(rows, "y", axis=0, tiled=True)
    half, half_f = call(
        halves_body, [part, piece], [k_arr, after(x_b, give), dy, x_f],
        scratch=[pltpu.SemaphoreType.DMA((3,))], n_smem=1, hbm_in=(1, 2, 3),
    )

    near = across(half)
    near, half_f, gathered = lax.optimization_barrier((near, half_f, gathered))
    weights = gathered.astype(BF16)
    far = on_chip(near)
    near_f = across(half_f)
    far_f = on_chip(near_f)

    grads, dgu = call(
        backward_body, [struct((16, 384, 128)), struct((384, 256))], [k_arr, gain, x_b, dy, near, far, weights],
        scratch=[
            pltpu.VMEM((384, 256), F32), pltpu.VMEM((384, 128), F32),
            pltpu.VMEM((384, 384), BF16), pltpu.VMEM((384, 2048), BF16), pltpu.VMEM((384, 2048), BF16),
            pltpu.VMEM((384, 2048), BF16),
            pltpu.VMEM((16, 384, 128), BF16), pltpu.SemaphoreType.DMA((6,)), pltpu.SemaphoreType.DMA((8,)),
        ],
        flops=4 * 384 * 384 * 2048, n_smem=1, hbm_in=(2, 3, 4), hbm_out=(0,),
    )
    received = exchange(grads.reshape(8, 2, 384, 128), "y")
    own_sum, give = call(
        sum_body, [struct((384, 128), F32), struct((384, 128))], [x_arr, received],
        scratch=[pltpu.VMEM((8, 2, 384, 128), BF16), pltpu.SemaphoreType.DMA((6,))],
        n_smem=1, hbm_in=(1,),
    )
    other_sum = across(give)

    e_keep, e_send = call(cotangent_body, [part, part], [dgu, weights], flops=2 * 384 * 256 * 2048)
    e_recv = on_chip(e_send)
    q_keep, q_send = call(
        forward_body, [part, part], [k_arr, gain, x_f, near_f, after(far_f, e_send), weights],
        scratch=[
            pltpu.VMEM((384, 256), F32), pltpu.VMEM((384, 128), BF16),
            pltpu.VMEM((384, 2048), BF16), pltpu.VMEM((384, 2048), BF16), pltpu.SemaphoreType.DMA((3,)),
        ],
        flops=2 * 384 * 384 * 2048, n_smem=1, hbm_in=(2,),
    )
    q_recv = on_chip(q_send)
    ahead = call(ahead_body, [piece, piece], [k_arr, x_f, q_keep, q_recv], n_smem=1)
    (e_pair,) = call(pair_body, [piece], [e_keep, e_recv])
    e_other = across(e_pair)
    (back,) = call(back_body, [piece], [k_arr, gain, x_b, dy, e_keep, e_recv, e_other], n_smem=1)

    def relay(x, distance, turn):
        moves = [(s, s + distance) for s in range(sections) if 0 <= s + distance < sections]
        axes = ("section", "xh")
        return lax.ppermute(x, axes, [(2 * s + h, 2 * t + (h ^ turn)) for s, t in moves for h in range(2)])

    next_parts = relay(ahead[0], 1, 0), relay(ahead[1], 1, 1)
    back_part = relay(back, -1, 0)
    (joined,) = call(add_body, [part], [*next_parts, back_part])
    next_rows, back_rows = call(
        rejoin_body, [part, part], [k_arr, joined, on_chip(joined)],
        scratch=[pltpu.SemaphoreType.DMA((4,))], n_smem=1, hbm_out=(0, 1),
    )

    rows_all = dy.shape[0] * lax.axis_size(DP)
    in_update, out_update = call(
        functools.partial(update_body, float(rows_all)),
        [struct((2, 128, 256), F32), struct((256, 128), F32)],
        [x_arr, own_sum, other_sum, c_in, s_in, c_out, s_out], n_smem=1,
    )
    return next_rows[None], back_rows[None], in_update[None], out_update[None]


def solution(mesh):
    split = Mesh(
        mesh.devices.reshape(mesh.shape["section"], 8, 2, mesh.shape["hid"]),
        ("section", "y", "xh", "hid"),
    )
    return jax.shard_map(
        tick,
        mesh=split,
        in_specs=(
            P("section", DP, None),
            P("section", DP, None),
            P("section", DP, None),
            P("section", None),
            P("section", None, DP, "hid"),
            P("section", "hid", DP),
            P("section", None, DP, "hid"),
            P("section", "hid", DP),
            P("section", None, None, DP, "hid"),
            P("section", None, "hid", DP),
            P("section"),
        ),
        out_specs=(
            P("section", DP, None),
            P("section", DP, None),
            P("section", None, DP, "hid"),
            P("section", "hid", DP),
        ),
        check_vma=False,
    )
```
